32 devices in a mesh: dp: 4 (over z), seq: 4 (over y, x), expert: 2 (over core).
Axes of the slice: x: 2, y: 2, z: 4, core: 2. Of those that a mesh axis runs over, the one named last changes fastest.
Arguments:
- block_input: float32 [8, 512, 768], P(('dp', 'expert'), 'seq'), may hold values from -12 to 12
- documents: int32 [8, 512], P(('dp', 'expert')), may hold values from 0 to 2, never falling along the last dimension, each value on 1 to 320 neighbouring positions
- route_experts: int32 [8, 512, 2], P(('dp', 'expert'), 'seq'), may hold values from 0 to 7, all different within a row; in each aligned block of 128 rows (0 to 127, 128 to 255, ..., all dimensions but the last counted through in order) at most 48 rows name the same one
- route_gate: float32 [8, 512, 2], P(('dp', 'expert'), 'seq'), may hold values from 0.25 to 1
- first_gain: bfloat16 [768], P(('dp', 'seq', 'expert')), may hold values from 0.25 to 1.75
- entry_weight: bfloat16 [768, 2304], P(None, ('dp', 'seq', 'expert')), may hold values from -0.21875 to 0.21875
- exit_weight: bfloat16 [768, 768], P(None, ('dp', 'seq', 'expert')), may hold values from -0.875 to 0.875
- position_bias: float32 [32, 12], replicated, may hold values from -4 to 260
- second_gain: bfloat16 [768], P(('dp', 'seq', 'expert')), may hold values from 0.25 to 1.75
- expert_up: bfloat16 [8, 768, 3072], P(('dp', 'expert'), None, 'seq'), may hold values from -0.21875 to 0.21875
- expert_down: bfloat16 [8, 3072, 768], P(('dp', 'expert'), 'seq'), may hold values from -0.109375 to 0.109375
- cotangent: float32 [8, 512, 768], P(('dp', 'expert'), 'seq'), may hold values from -6 to 6
Outputs:
- block_output: float32 [8, 512, 768], P(('dp', 'expert'), 'seq')
- back_input: float32 [8, 512, 768], P(('dp', 'expert'), 'seq')
- back_first_gain: float32 [768], P(('dp', 'seq', 'expert'))
- back_entry: float32 [768, 2304], P(None, ('dp', 'seq', 'expert'))
- back_exit: float32 [768, 768], P(None, ('dp', 'seq', 'expert'))
- back_bias: float32 [32, 12], replicated
- back_second_gain: float32 [768], P(('dp', 'seq', 'expert'))
- back_expert_up: float32 [8, 768, 3072], P(('dp', 'expert'), None, 'seq')
- back_expert_down: float32 [8, 3072, 768], P(('dp', 'expert'), 'seq')
The draws below stay inside these ranges and needn't reach their ends.
Inputs may be any that keep to these rules, and one draw needn't show every extreme that they name: `route_experts`: in each device's aligned block of 128 tokens no expert is named by more than 48 routes, a bound that some block reaches; a token's two experts differ. `documents`: document numbers never fall along a sequence; no document is longer than five eighths of 512 tokens, and one is that long.
All inputs are finite; a program needn't handle non-finite values.
Results may differ from the reference program's by a relative error of at most 0.014.
Values may be sent and summed in bfloat16 or wider, within the bound.
No kernel may reach another device: no remote copies, remote signals or barrier semaphores. Data moves between devices by JAX's collectives and lax.ppermute only.
A program may use at most 128 MiB of HBM per device.

```python
import math
import jax
import jax.numpy as jnp
import numpy as np
from jax import lax

D = 768
HEADS = 12
HEAD_DIM = 64
FF = 3072
NBUCKET = 32
TOP = 2
TOK_DEV = 128
LENGTH = 512
SEQS = 8
EXPERTS = 8
CAP = 48
N_DP = 4
N_SEQ = 4
N_EXPERT = 2


def draw_block_input(key, part):
    first, second, third = jax.random.split(key, 3)
    low = -0.5 * math.log(10.0)
    high = 0.5 * math.log(10.0)
    row_scale = jnp.exp(jax.random.uniform(second, (SEQS, LENGTH, 1), jnp.float32, low, high))
    column_scale = jnp.exp(jax.random.uniform(third, (1, 1, D), jnp.float32, low, high))
    base = jax.random.truncated_normal(first, -4.0, 4.0, (SEQS, LENGTH, D), jnp.float32)
    return 0.3 * base * row_scale * column_scale


def draw_position_bias(key, part):
    first = jax.random.fold_in(key, 0)
    return 0.5 * jax.random.truncated_normal(first, -4.0, 4.0, (NBUCKET, HEADS), jnp.float32)


def raised(drawn, rng, source, target, parts, factor):
    owner, partner = [(jnp.arange(drawn.shape[position]) // (drawn.shape[position] // parts)).reshape([-1 if axis == position else 1 for axis in range(drawn.ndim)]) for position in (source, target)]
    chosen = jax.random.permutation(rng, parts)[partner]
    strong = (owner == chosen) | (owner == (partner + parts // 2) % parts)
    return jnp.where(strong, factor * drawn, drawn)


def block_levels(rng, extent, shards, low, top_value):
    loudness = 1.0
    for position, blocks in shards:
        heights = jax.random.uniform(jax.random.fold_in(jax.random.fold_in(rng, 6), position), (blocks,), jnp.float32, low / len(shards), top_value / len(shards))
        loudness = loudness * jnp.repeat(jnp.exp(heights), extent[position] // blocks).reshape((-1,) + (1,) * (len(extent) - 1 - position))
    return loudness


def length_profile(count, total, limit, slope):
    portions = [(1 << 20) // math.isqrt(rank ** slope) + 1 for rank in range(2, count + 1)]
    rest, given = total - limit - (count - 1), [1] * (count - 1)
    while rest > 0:
        movable = [i for i in range(count - 1) if given[i] < limit]
        whole, budget = sum([portions[i] for i in movable]), rest
        for i in movable:
            addition = min(limit - given[i], max(1, budget * portions[i] // whole), rest)
            given[i] = given[i] + addition
            rest = rest - addition
    return np.array([limit] + given)


def ragged(stream_key, number_of, total, bound, skew):
    if number_of == 2:
        one = jax.random.randint(stream_key, (), max(1, total - bound), min(bound, total - 1) + 1)
        return jnp.stack([one, total - one])
    lengths = jnp.asarray(length_profile(number_of, total, bound, skew), jnp.int32)
    couples = (number_of - 1) // 2
    source_of, taker = lengths[1:1 + 2 * couples:2], lengths[2:2 + 2 * couples:2]
    margin = jnp.minimum(source_of - 1, bound - taker)
    passed = jax.random.randint(jax.random.fold_in(stream_key, 1), (couples,), 0, 1 << 20) % (margin + 1)
    lengths = lengths.at[1:1 + 2 * couples:2].set(source_of - passed).at[2:2 + 2 * couples:2].set(taker + passed)
    return lengths[jax.random.permutation(jax.random.fold_in(stream_key, 2), number_of)]


def assign_block(stream_key, own, number, rows, amount, top, most, lean):
    sequence = jax.random.permutation(stream_key, amount)
    crowded, common = shares(amount, rows * top, most, lean, True), shares(amount, rows * top, most, lean, False)
    places = jnp.arange(amount)

    def named(sizes, rotation):
        used = int((sizes > 0).sum())
        fixed = max(1, used // 4)
        moved = fixed + (places - fixed + rotation * (used - fixed)) % max(1, amount - fixed)
        return jnp.zeros((amount,), jnp.int32).at[sequence[jnp.where(places < fixed, places, moved)]].set(jnp.asarray(sizes, jnp.int32))

    sizes = jnp.where(number % 4 == 0, named(crowded, number // 4), named(common, number - number // 4 - 1))
    mixed = jax.random.permutation(jax.random.fold_in(own, 3), amount)
    source_of, receiver = mixed[0:amount // 2 * 2:2], mixed[1:amount // 2 * 2:2]
    slack = jnp.minimum(sizes[source_of] - 1, most - sizes[receiver]) // 2
    slack = jnp.where((source_of == sequence[0]) | (receiver == sequence[0]) | (sizes[receiver] == 0), 0, jnp.maximum(slack, 0))
    moved = jax.random.randint(jax.random.fold_in(own, 4), (amount // 2,), 0, 1 << 20) % (slack + 1)
    sizes = sizes.at[source_of].add(-moved).at[receiver].add(moved)
    items = jnp.searchsorted(jnp.cumsum(sizes), jnp.arange(rows * top), side="right").astype(jnp.int32)
    listing = items.reshape(top, rows).T
    listing = listing[jax.random.permutation(jax.random.fold_in(own, 1), rows)]
    rotation = jax.random.randint(jax.random.fold_in(own, 2), (rows, 1), 0, top)
    return jnp.take_along_axis(listing, (jnp.arange(top)[None, :] + rotation) % top, axis=1)


def shares(number_of, total, bound, lean, full):
    portions = [(1 << 20) // math.isqrt(grade ** lean) + 1 for grade in range(1, number_of + 1)]
    largest = bound if full else min(bound, max(-(-total // number_of), total * portions[0] // sum(portions)))
    least = 1 if total - largest >= number_of - 1 else 0
    given, rest = [largest] + [least] * (number_of - 1), total - largest - least * (number_of - 1)
    while rest > 0:
        candidates = [i for i in range(1, number_of) if given[i] < largest] or [i for i in range(1, number_of) if given[i] < bound]
        whole, left = sum([portions[i] for i in candidates]), rest
        for i in candidates:
            more = min(bound - given[i], max(1, left * portions[i] // whole), rest)
            given[i] = given[i] + more
            rest = rest - more
    return np.array(given)


def gaussian(rng, shape, scale, limit, cuts=(), kind=jnp.bfloat16):
    drawn = scale * jax.random.normal(rng, shape, jnp.float32)
    if cuts:
        drawn = drawn * block_levels(rng, shape, cuts, -0.22, 0.18)
    return jnp.clip(drawn, -limit, limit).astype(kind)


def bell_draw_with(own_key, shape, scale, bound, cuts, heavy, held_as=jnp.bfloat16):
    entries = scale * jax.random.normal(own_key, shape, jnp.float32)
    if cuts:
        entries = entries * block_levels(own_key, shape, cuts, -0.22, 0.18)
    return jnp.clip(raised(entries, jax.random.fold_in(own_key, 3), *heavy), -bound, bound).astype(held_as)


def setup_inputs(seed: int = 0) -> dict:
    key_list = jax.random.split(jax.random.key(seed), 13)
    block_input = draw_block_input(jax.random.fold_in(key_list[12], 71), 0)
    documents = jax.vmap(lambda own: jnp.searchsorted(jnp.cumsum(ragged(own, 3, LENGTH, LENGTH * 5 // 8, 0)), jnp.arange(LENGTH), side="right"))(jax.random.split(key_list[1], SEQS)).reshape((SEQS, LENGTH)).astype(jnp.int32)
    route_experts_keys = jax.random.split(jax.random.fold_in(key_list[2], 1), SEQS * LENGTH // TOK_DEV)
    route_experts_turns = jax.random.permutation(jax.random.fold_in(key_list[2], 3), SEQS * LENGTH // TOK_DEV)
    route_experts = jax.vmap(lambda own, number: assign_block(jax.random.fold_in(key_list[2], 2), own, number, TOK_DEV, EXPERTS, TOP, CAP, 1))(route_experts_keys, route_experts_turns).reshape((SEQS, LENGTH, TOP))
    route_gate = jnp.clip(0.25 + 0.75 * jax.random.uniform(key_list[3], (SEQS, LENGTH, TOP), jnp.float32) ** block_levels(key_list[3], (SEQS, LENGTH, TOP), ((0, 8), (1, 4)), -0.2, 0.2), 0.25, 1.0)
    first_gain = jnp.clip(1.0 + 0.15 * jax.random.normal(key_list[4], (D,), jnp.float32), 0.25, 1.75).astype(jnp.bfloat16)
    entry_weight = gaussian(key_list[5], (D, 3 * D), D ** -0.5, 0.21875, ((1, 32),))
    exit_weight = gaussian(key_list[6], (D, D), (D // 16) ** -0.5, 0.875, ((1, 32),))
    position_bias = draw_position_bias(jax.random.fold_in(key_list[12], 71), 0)
    second_gain = jnp.clip(1.0 + 0.15 * jax.random.normal(key_list[8], (D,), jnp.float32), 0.25, 1.75).astype(jnp.bfloat16)
    expert_up = gaussian(key_list[9], (EXPERTS, D, FF), D ** -0.5, 0.21875, ((0, 8), (2, 4)))
    expert_down = gaussian(key_list[10], (EXPERTS, FF, D), FF ** -0.5, 0.109375, ((0, 8), (1, 4)))
    cotangent = bell_draw_with(key_list[11], (SEQS, LENGTH, D), 1.0, 6.0, ((0, 8), (1, 4)), (0, 2, 8, 2.0), jnp.float32)
    return {"block_input": block_input, "documents": documents, "route_experts": route_experts, "route_gate": route_gate, "first_gain": first_gain, "entry_weight": entry_weight, "exit_weight": exit_weight, "position_bias": position_bias, "second_gain": second_gain, "expert_up": expert_up, "expert_down": expert_down, "cotangent": cotangent}


EPSILON = 1e-06
SLOPE = 0.7978845608028654
CUBIC = 0.044715
LIMITS = (19, 21, 24, 27, 31, 35, 40, 46, 52, 59, 67, 77, 87, 99, 113)
MASKED = -1e+30
HIGH = lax.Precision.HIGHEST

def gelu_value(values):
    return 0.5 * values * (1.0 + jnp.tanh(SLOPE * (values + CUBIC * values * values * values)))

def gelu_slope(values):
    tangent = jnp.tanh(SLOPE * (values + CUBIC * values * values * values))
    return 0.5 * (1.0 + tangent) + 0.5 * values * (1.0 - tangent * tangent) * SLOPE * (1.0 + 3.0 * CUBIC * values * values)

def bucket_onehot(lag, count):
    bucket = jnp.minimum(lag, 16)
    for threshold in LIMITS:
        bucket = bucket + (lag >= threshold).astype(jnp.int32)
    return (bucket[..., None] == jnp.arange(count, dtype=jnp.int32)).astype(jnp.float32)

def rms_scale(values):
    return lax.rsqrt(lax.optimization_barrier(jnp.mean(values * values, axis=-1, keepdims=True)) + EPSILON)

def expert_work(rows, upstream, up_weight, down_weight):
    before = jnp.dot(rows, up_weight, preferred_element_type=jnp.float32)
    active = gelu_value(before).astype(jnp.bfloat16)
    result = jnp.dot(active, down_weight, preferred_element_type=jnp.float32)
    back_active = jnp.dot(upstream, down_weight.T, preferred_element_type=jnp.float32)
    back_before = (back_active * gelu_slope(before)).astype(jnp.bfloat16)
    down_grad = jnp.dot(active.T, upstream, preferred_element_type=jnp.float32)
    up_grad = jnp.dot(rows.T, back_before, preferred_element_type=jnp.float32)
    back_rows = jnp.dot(back_before, up_weight.T, preferred_element_type=jnp.float32)
    return (result, back_rows, up_grad, down_grad)

def reference(block_input, documents, route_experts, route_gate, first_gain, entry_weight, exit_weight, position_bias, second_gain, expert_up, expert_down, cotangent):
    factor = HEAD_DIM ** (-0.5)
    gain_one = first_gain.astype(jnp.float32)
    gain_two = second_gain.astype(jnp.float32)
    places = jnp.arange(LENGTH, dtype=jnp.int32)
    bucket_hot = bucket_onehot(jnp.maximum(places[:, None] - places[None, :], 0), NBUCKET)
    bias_block = jnp.einsum('qkb,bh->hqk', bucket_hot, position_bias, precision=HIGH)
    causal = places[None, :] <= places[:, None]

    def score_of(projected, allowed):
        queries = projected[:, :D].reshape(LENGTH, HEADS, HEAD_DIM).astype(jnp.float32)
        key_heads = projected[:, D:2 * D].reshape(LENGTH, HEADS, HEAD_DIM).astype(jnp.float32)
        scores = jnp.einsum('qhd,khd->hqk', queries, key_heads) * factor + bias_block
        return jnp.where(allowed[None], scores, MASKED)

    def forward_one(pieces):
        inputs, segment_row = pieces
        allowed = causal & (segment_row[:, None] == segment_row[None, :])
        scale_one = rms_scale(inputs)
        normed_one = (inputs * scale_one * gain_one).astype(jnp.bfloat16)
        projected = jnp.dot(normed_one, entry_weight, preferred_element_type=jnp.float32).astype(jnp.bfloat16)
        scores = score_of(projected, allowed)
        row_peak = lax.optimization_barrier(jnp.max(scores, axis=2, keepdims=True))
        log_total = row_peak + jnp.log(lax.optimization_barrier(jnp.sum(jnp.exp(scores - row_peak), axis=2, keepdims=True)))
        weights = jnp.where(allowed[None], jnp.exp(scores - log_total), 0.0).astype(jnp.bfloat16)
        values = projected[:, 2 * D:].reshape(LENGTH, HEADS, HEAD_DIM).astype(jnp.float32)
        context = jnp.einsum('hqk,khd->qhd', weights.astype(jnp.float32), values).astype(jnp.bfloat16).reshape(LENGTH, D)
        hidden = inputs + jnp.dot(context, exit_weight, preferred_element_type=jnp.float32)
        return (hidden, normed_one, projected, context, log_total)
    hidden, normed_one, projected, context, log_total = lax.map(forward_one, (block_input, documents))
    total = SEQS * LENGTH
    flat_hidden = hidden.reshape(total, D)
    scale_two = rms_scale(flat_hidden)
    normed_two = (flat_hidden * scale_two * gain_two).astype(jnp.bfloat16)
    upstream = cotangent.reshape(total, D)
    flat_routes = route_experts.reshape(total * TOP).astype(jnp.int32)
    flat_gates = route_gate.reshape(total * TOP)
    order = jnp.argsort(flat_routes, stable=True).astype(jnp.int32)
    counts = lax.optimization_barrier(jnp.sum((flat_routes[:, None] == jnp.arange(EXPERTS, dtype=jnp.int32)[None, :]).astype(jnp.int32), axis=0))
    starts = (jnp.cumsum(counts) - counts).astype(jnp.int32)
    most_rows = CAP * N_DP * N_SEQ * N_EXPERT
    padded = jnp.concatenate([order, jnp.zeros((most_rows,), jnp.int32)])

    def one_expert(index):
        picked = lax.dynamic_slice_in_dim(padded, starts[index], most_rows)
        live = jnp.arange(most_rows, dtype=jnp.int32) < counts[index]
        token_ids = picked // TOP
        rows = normed_two[token_ids]
        route_up = jnp.where(live[:, None], upstream[token_ids] * flat_gates[picked][:, None], 0.0).astype(jnp.bfloat16)
        result, back_rows, up_grad, down_grad = expert_work(rows, route_up, expert_up[index], expert_down[index])
        target = jnp.where(live, picked, total * TOP).astype(jnp.int32)
        return (result.astype(jnp.bfloat16), back_rows.astype(jnp.bfloat16), target, up_grad, down_grad)
    results, backs, targets, up_grads, down_grads = lax.map(one_expert, jnp.arange(EXPERTS, dtype=jnp.int32))
    flat_targets = targets.reshape(-1)
    route_out = jnp.zeros((total * TOP + 1, D), jnp.bfloat16).at[flat_targets].set(results.reshape(-1, D))[:total * TOP]
    route_back = jnp.zeros((total * TOP + 1, D), jnp.bfloat16).at[flat_targets].set(backs.reshape(-1, D))[:total * TOP]
    mixture = lax.optimization_barrier(jnp.sum(route_out.astype(jnp.float32).reshape(total, TOP, D) * flat_gates.reshape(total, TOP, 1), axis=1))
    block_output = (flat_hidden + mixture).reshape(SEQS, LENGTH, D)
    back_normed_two = lax.optimization_barrier(jnp.sum(route_back.astype(jnp.float32).reshape(total, TOP, D), axis=1))
    upper_two = back_normed_two * gain_two
    back_second_gain = lax.optimization_barrier(jnp.sum(back_normed_two * flat_hidden * scale_two, axis=0))
    back_hidden = upstream + scale_two * (upper_two - flat_hidden * scale_two * scale_two * lax.optimization_barrier(jnp.mean(upper_two * flat_hidden, axis=1, keepdims=True)))
    back_hidden = back_hidden.reshape(SEQS, LENGTH, D)

    def backward_one(carry, pieces):
        entry_sum, exit_sum, bias_sum, gain_sum = carry
        inputs, segment_row, normed_seq, projected_seq, context_seq, total_seq, hidden_back = pieces
        allowed = causal & (segment_row[:, None] == segment_row[None, :])
        upstream_hidden = hidden_back.astype(jnp.bfloat16)
        exit_sum = exit_sum + jnp.dot(context_seq.T, upstream_hidden, preferred_element_type=jnp.float32)
        back_context = jnp.dot(upstream_hidden, exit_weight.T, preferred_element_type=jnp.float32).astype(jnp.bfloat16).reshape(LENGTH, HEADS, HEAD_DIM).astype(jnp.float32)
        scores = score_of(projected_seq, allowed)
        probs = jnp.where(allowed[None], jnp.exp(scores - total_seq), 0.0)
        values = projected_seq[:, 2 * D:].reshape(LENGTH, HEADS, HEAD_DIM).astype(jnp.float32)
        queries = projected_seq[:, :D].reshape(LENGTH, HEADS, HEAD_DIM).astype(jnp.float32)
        key_heads = projected_seq[:, D:2 * D].reshape(LENGTH, HEADS, HEAD_DIM).astype(jnp.float32)
        back_probs = jnp.einsum('qhd,khd->hqk', back_context, values)
        row_dot = lax.optimization_barrier(jnp.sum(probs * back_probs, axis=2, keepdims=True))
        back_scores = probs * (back_probs - row_dot)
        bias_sum = bias_sum + jnp.einsum('hqk,qkb->bh', back_scores, bucket_hot, precision=HIGH)
        scaled_back = (back_scores * factor).astype(jnp.bfloat16).astype(jnp.float32)
        back_queries = jnp.einsum('hqk,khd->qhd', scaled_back, key_heads).reshape(LENGTH, D)
        back_keys = jnp.einsum('hqk,qhd->khd', scaled_back, queries).reshape(LENGTH, D)
        weights = probs.astype(jnp.bfloat16).astype(jnp.float32)
        back_values = jnp.einsum('hqk,qhd->khd', weights, back_context).reshape(LENGTH, D)
        back_projected = jnp.concatenate([back_queries, back_keys, back_values], axis=1).astype(jnp.bfloat16)
        entry_sum = entry_sum + jnp.dot(normed_seq.T, back_projected, preferred_element_type=jnp.float32)
        back_normed_one = jnp.dot(back_projected, entry_weight.T, preferred_element_type=jnp.float32)
        scale_one = rms_scale(inputs)
        upper_one = back_normed_one * gain_one
        gain_sum = gain_sum + lax.optimization_barrier(jnp.sum(back_normed_one * inputs * scale_one, axis=0))
        back_seq = hidden_back + scale_one * (upper_one - inputs * scale_one * scale_one * lax.optimization_barrier(jnp.mean(upper_one * inputs, axis=1, keepdims=True)))
        return ((entry_sum, exit_sum, bias_sum, gain_sum), back_seq)
    start = (jnp.zeros((D, 3 * D), jnp.float32), jnp.zeros((D, D), jnp.float32), jnp.zeros((NBUCKET, HEADS), jnp.float32), jnp.zeros((D,), jnp.float32))
    sums, back_input = lax.scan(backward_one, start, (block_input, documents, normed_one, projected, context, log_total, back_hidden))
    back_entry, back_exit, back_bias, back_first_gain = sums
    return (block_output, back_input, back_first_gain, back_entry, back_exit, back_bias, back_second_gain, up_grads, down_grads)
```

```python
import functools
import math

import jax
import jax.numpy as jnp
import numpy as np
from jax import lax
from jax.experimental import pallas as pl
from jax.experimental.pallas import tpu as pltpu
from jax.sharding import PartitionSpec as P

EPSILON = 1e-06
SLOPE = 0.7978845608028654
CUBIC = 0.044715
LIMITS = (19, 21, 24, 27, 31, 35, 40, 46, 52, 59, 67, 77, 87, 99, 113)
MASKED = -1e30
HIGH = lax.Precision.HIGHEST
ALL = ("dp", "seq", "expert")
GROUP = ("dp", "expert")
BLOCK = 128
BF = jnp.bfloat16
F32 = jnp.float32


def dot(left, right, left_dim, right_dim):
    return lax.dot_general(
        left, right, (((left_dim,), (right_dim,)), ((), ())), preferred_element_type=F32
    )


def rms_scale(values):
    return lax.rsqrt(jnp.mean(values * values, axis=-1, keepdims=True) + EPSILON)


def bucket_hot(lag, count):
    bucket = jnp.minimum(lag, 16)
    for threshold in LIMITS:
        bucket = bucket + (lag >= threshold).astype(jnp.int32)
    return (jnp.arange(count, dtype=jnp.int32)[:, None] == bucket[None, :]).astype(F32)


@functools.lru_cache(maxsize=None)
def weight_routes(features, columns, n_dp, n_seq, n_ex):
    width = features // n_seq
    chunk = math.gcd(columns, width)
    per = columns // chunk
    devices = n_dp * n_seq * n_ex
    edges = []
    for group in range(n_seq):
        index = 0
        for part in range(3):
            for i in range(width // chunk):
                piece = (part * features + group * width) // chunk + i
                ex, rest = divmod(index, n_dp * per)
                dp, slot = divmod(rest, per)
                target = (dp * n_seq + group) * n_ex + ex
                edges.append((piece // per, piece % per, target, slot))
                index += 1
    rounds = []
    left = list(edges)
    for _ in range(per):
        out_edges = [[] for _ in range(devices)]
        for edge in left:
            out_edges[edge[0]].append(edge)
        matched = {}

        def place(source, seen):
            for edge in out_edges[source]:
                if edge[2] in seen:
                    continue
                seen.add(edge[2])
                if edge[2] not in matched or place(matched[edge[2]][0], seen):
                    matched[edge[2]] = edge
                    return True
            return False

        for source in range(devices):
            assert place(source, set())
        rounds.append(sorted(matched.values()))
        for edge in matched.values():
            left.remove(edge)
    pairs = tuple(tuple((e[0], e[2]) for e in r) for r in rounds)
    send = np.zeros((devices, per), np.int32)
    receive = np.zeros((devices, per), np.int32)
    for m, r in enumerate(rounds):
        for source, sub, target, slot in r:
            send[source, m] = sub
            receive[target, slot] = m
    return chunk, per, pairs, send, receive


def inverse_rows(table):
    return np.argsort(table, axis=1).astype(np.int32)


def pick(stack, table, me):
    row = jnp.asarray(table)[me]
    return [
        lax.dynamic_index_in_dim(stack, row[j], axis=0, keepdims=False)
        for j in range(table.shape[1])
    ]


def spread_out(array, axis):
    count = lax.axis_size(axis)
    return lax.all_to_all(
        jnp.broadcast_to(array[None], (count,) + array.shape), axis, 0, 0, tiled=True
    )


def allowed_of(docs_row, docs_col, start, rows, keys):
    query = start + lax.broadcasted_iota(jnp.int32, (rows, keys), 0)
    key = lax.broadcasted_iota(jnp.int32, (rows, keys), 1)
    return (key <= query) & (docs_col[start : start + rows, :] == docs_row[:, :keys])


def bias_rows(lag_ref, head, start, rows, keys):
    length = lag_ref.shape[1]
    flat = jnp.broadcast_to(lag_ref[head : head + 1, :], (rows, length))
    return pltpu.roll(flat, start, 1, stride=1, stride_axis=0)[:, :keys]


def attend_kernel(
    heads, size, x_ref, gain_ref, w_ref, exit_ref, row_ref, col_ref, lag_ref,
    qkv_ref, ctx_ref, log_ref, part_ref,
):
    length = x_ref.shape[0]
    width = heads * size
    factor = size ** (-0.5)
    normed = (x_ref[...].astype(F32) * gain_ref[...]).astype(BF)
    qkv_ref[...] = dot(normed, w_ref[...], 1, 1).astype(BF)
    for start in range(0, length, BLOCK):
        keys = start + BLOCK
        allowed = allowed_of(row_ref, col_ref, start, BLOCK, keys)
        for head in range(heads):
            lo = head * size
            q = qkv_ref[start:keys, lo : lo + size]
            k = qkv_ref[:keys, width + lo : width + lo + size]
            v = qkv_ref[:keys, 2 * width + lo : 2 * width + lo + size]
            scores = dot(q, k, 1, 1) * factor + bias_rows(lag_ref, head, start, BLOCK, keys)
            scores = jnp.where(allowed, scores, MASKED)
            peak = jnp.max(scores, axis=1, keepdims=True)
            raised = jnp.exp(scores - peak)
            total = jnp.sum(raised, axis=1, keepdims=True)
            weights = (raised / total).astype(BF)
            log_ref[start:keys, head : head + 1] = peak + jnp.log(total)
            ctx_ref[start:keys, lo : lo + size] = dot(weights, v, 1, 0).astype(BF)
    part_ref[...] = dot(ctx_ref[...], exit_ref[...], 1, 1).astype(BF)


def attend(heads, size, xhat, gain, w, exit_t, docs_row, docs_col, lag):
    length, features = xhat.shape
    width = heads * size
    return pl.pallas_call(
        functools.partial(attend_kernel, heads, size),
        out_shape=(
            jax.ShapeDtypeStruct((length, 3 * width), BF),
            jax.ShapeDtypeStruct((length, width), BF),
            jax.ShapeDtypeStruct((length, heads), F32),
            jax.ShapeDtypeStruct((length, features), BF),
        ),
        name="attend",
    )(xhat, gain, w, exit_t, docs_row, docs_col, lag)


def attend_back_kernel(
    heads, size, up_ref, exit_ref, qkv_ref, ctx_ref, log_ref, row_ref, col_ref, lag_ref,
    x_ref, gain_ref, w_ref,
    entry_ref, exit_grad_ref, back_ref, diag_ref, gain_grad_ref,
    bctx_ref, bqkv_ref, bk_ref, bv_ref, lines_ref,
):
    length = up_ref.shape[0]
    width = heads * size
    factor = size ** (-0.5)
    bctx_ref[...] = dot(up_ref[...], exit_ref[...], 1, 0).astype(BF)
    exit_grad_ref[...] = dot(up_ref[...], ctx_ref[...], 0, 0).astype(BF)
    bk_ref[...] = jnp.zeros_like(bk_ref)
    bv_ref[...] = jnp.zeros_like(bv_ref)
    lines_ref[...] = jnp.zeros_like(lines_ref)
    for start in range(0, length, BLOCK):
        keys = start + BLOCK
        allowed = allowed_of(row_ref, col_ref, start, BLOCK, keys)
        for head in range(heads):
            lo = head * size
            q = qkv_ref[start:keys, lo : lo + size]
            k = qkv_ref[:keys, width + lo : width + lo + size]
            v = qkv_ref[:keys, 2 * width + lo : 2 * width + lo + size]
            bc = bctx_ref[start:keys, lo : lo + size]
            scores = dot(q, k, 1, 1) * factor + bias_rows(lag_ref, head, start, BLOCK, keys)
            probs = jnp.where(
                allowed, jnp.exp(scores - log_ref[start:keys, head : head + 1]), 0.0
            )
            back_probs = dot(bc, v, 1, 1)
            row_dot = jnp.sum(probs * back_probs, axis=1, keepdims=True)
            back_scores = probs * (back_probs - row_dot)
            scaled = (back_scores * factor).astype(BF)
            bqkv_ref[start:keys, lo : lo + size] = dot(scaled, k, 1, 0).astype(BF)
            bk_ref[:keys, lo : lo + size] += dot(scaled, q, 0, 0)
            bv_ref[:keys, lo : lo + size] += dot(probs.astype(BF), bc, 0, 0)
            lined = jnp.zeros((8, keys), F32)
            for row in range(0, BLOCK, 8):
                lined = lined + pltpu.roll(
                    back_scores[row : row + 8, :], (keys - start - row - 8) % keys, 1
                )
            lines_ref[8 * head : 8 * head + 8, length - keys :] += lined
    for head in range(heads):
        total = jnp.zeros((1, length), F32)
        for row in range(8):
            total = total + pltpu.roll(
                lines_ref[8 * head + row : 8 * head + row + 1, :], 7 - row, 1
            )
        diag_ref[head : head + 1, :] = total
    bqkv_ref[:, width : 2 * width] = bk_ref[...].astype(BF)
    bqkv_ref[:, 2 * width :] = bv_ref[...].astype(BF)
    normed = (x_ref[...].astype(F32) * gain_ref[...]).astype(BF)
    entry_ref[...] = dot(bqkv_ref[...], normed, 0, 0).astype(BF)
    back = dot(bqkv_ref[...], w_ref[...], 1, 0)
    back_ref[...] = back.astype(BF)
    gain_grad_ref[...] = jnp.sum(back * x_ref[...].astype(F32), axis=0, keepdims=True)


def attend_back(heads, size, up, exit_t, qkv, ctx, log, docs_row, docs_col, lag, xhat, gain, w):
    length, features = up.shape
    width = heads * size
    return pl.pallas_call(
        functools.partial(attend_back_kernel, heads, size),
        out_shape=(
            jax.ShapeDtypeStruct((3 * width, features), BF),
            jax.ShapeDtypeStruct((features, width), BF),
            jax.ShapeDtypeStruct((length, features), BF),
            jax.ShapeDtypeStruct((heads, length), F32),
            jax.ShapeDtypeStruct((1, features), F32),
        ),
        scratch_shapes=[
            pltpu.VMEM((length, width), BF),
            pltpu.VMEM((length, 3 * width), BF),
            pltpu.VMEM((length, width), F32),
            pltpu.VMEM((length, width), F32),
            pltpu.VMEM((8 * heads, length), F32),
        ],
        name="attend_back",
    )(up, exit_t, qkv, ctx, log, docs_row, docs_col, lag, xhat, gain, w)


def expert_kernel(rows_ref, up_ref, w_up_ref, w_down_ref, back_ref, result_ref, act_ref, bb_ref):
    before = dot(rows_ref[...], w_up_ref[...], 1, 0)
    tangent = jnp.tanh(SLOPE * (before + CUBIC * before * before * before))
    act_ref[...] = (0.5 * before * (1.0 + tangent)).astype(BF)
    slope = 0.5 * (1.0 + tangent) + 0.5 * before * (1.0 - tangent * tangent) * SLOPE * (
        1.0 + 3.0 * CUBIC * before * before
    )
    bb_ref[...] = (dot(up_ref[...], w_down_ref[...], 1, 1) * slope).astype(BF)
    back_ref[...] = dot(bb_ref[...], w_up_ref[...], 1, 1).astype(BF)
    result_ref[...] = dot(act_ref[...], w_down_ref[...], 1, 0).astype(BF)


def expert(rows, upstream, w_up, w_down):
    count, features = rows.shape
    hidden = w_up.shape[1]
    return pl.pallas_call(
        expert_kernel,
        out_shape=(
            jax.ShapeDtypeStruct((count, features), BF),
            jax.ShapeDtypeStruct((count, features), BF),
            jax.ShapeDtypeStruct((count, hidden), BF),
            jax.ShapeDtypeStruct((count, hidden), BF),
        ),
        name="expert",
    )(rows, upstream, w_up, w_down)


def expert_grad_kernel(count, *refs):
    rows, bbs = refs[:count], refs[count : 2 * count]
    acts, ups = refs[2 * count : 3 * count], refs[3 * count : 4 * count]
    up_ref, down_ref = refs[4 * count :]
    total = dot(rows[0][...], bbs[0][...], 0, 0)
    for i in range(1, count):
        total = total + dot(rows[i][...], bbs[i][...], 0, 0)
    up_ref[...] = total
    total = dot(acts[0][...], ups[0][...], 0, 0)
    for i in range(1, count):
        total = total + dot(acts[i][...], ups[i][...], 0, 0)
    down_ref[...] = total


def expert_grad(rows, bbs, acts, ups):
    features, hidden = rows[0].shape[1], bbs[0].shape[1]
    return pl.pallas_call(
        functools.partial(expert_grad_kernel, len(rows)),
        out_shape=(
            jax.ShapeDtypeStruct((features, hidden), F32),
            jax.ShapeDtypeStruct((hidden, features), F32),
        ),
        name="expert_grad",
    )(*rows, *bbs, *acts, *ups)


def ring(count, step):
    if count & (count - 1) == 0:
        return tuple((i, i ^ step) for i in range(count))
    return tuple((i, (i + step) % count) for i in range(count))


def back_ring(count, step):
    return tuple((b, a) for a, b in ring(count, step))


def local(
    block_input,
    documents,
    route_experts,
    route_gate,
    first_gain,
    entry_weight,
    exit_weight,
    position_bias,
    second_gain,
    expert_up,
    expert_down,
    cotangent,
):
    n_dp, n_seq, n_ex = (lax.axis_size(name) for name in ALL)
    devices = n_dp * n_seq * n_ex
    rows_here, features = block_input.shape[1:]
    buckets, head_count = position_bias.shape
    size = features // head_count
    heads = head_count // n_seq
    width = heads * size
    top_count = route_experts.shape[2]
    length = rows_here * n_seq
    me = lax.axis_index(ALL)
    here = lax.axis_index("seq")
    inputs = block_input.reshape(rows_here, features)
    upstream = cotangent.reshape(rows_here, features)

    owned = entry_weight.shape[1]
    share = exit_weight.shape[1]
    chunk, per, pairs, send, receive = weight_routes(features, owned, n_dp, n_seq, n_ex)
    pieces = pick(entry_weight.T.reshape(per, chunk, features), send, me)
    came = [lax.ppermute(piece, ALL, pair) for piece, pair in zip(pieces, pairs)]
    entry_mine = jnp.concatenate(pick(jnp.stack(came), receive, me), axis=0)
    entry_half = spread_out(entry_mine, "dp").reshape(n_dp * owned, features)
    entry_t = lax.all_gather(entry_half, "expert", axis=0, tiled=True)

    extra = -(-2 * share // width)
    gains = jnp.concatenate([first_gain, second_gain])
    gains = jnp.pad(gains, (0, extra * width - 2 * share)).reshape(1, extra, width)
    exit_send = jnp.concatenate(
        [
            exit_weight.T.reshape(share, n_seq, width).transpose(1, 0, 2),
            jnp.broadcast_to(gains, (n_seq, extra, width)),
        ],
        axis=1,
    )
    exit_send = jnp.broadcast_to(
        exit_send[None, :, None], (n_dp, n_seq, n_ex, share + extra, width)
    ).reshape(devices, share + extra, width)
    exit_came = lax.all_to_all(exit_send, ALL, 0, 0, tiled=True)
    exit_t = exit_came[:, :share].reshape(features, width)
    gains = exit_came[:, share:].reshape(devices, extra * width).astype(F32)
    gain_one = gains[:, :share].reshape(1, features)
    gain_two = gains[:, share : 2 * share].reshape(1, features)

    scale_one = rms_scale(inputs)
    xhat = spread_out((inputs * scale_one).astype(BF), "seq").reshape(length, features)
    docs = documents.reshape(length)
    docs_row, docs_col = docs.reshape(1, length), docs.reshape(length, 1)
    lane = jnp.arange(length, dtype=jnp.int32)
    hot = bucket_hot(jnp.where(lane == 0, 0, length - lane), buckets)
    bias_here = lax.dynamic_slice_in_dim(position_bias.T, here * heads, heads)
    lag = jnp.dot(bias_here, hot, precision=HIGH)
    qkv, ctx, log, part = attend(
        heads, size, xhat, gain_one, entry_t, exit_t, docs_row, docs_col, lag
    )

    group_size = n_dp * n_ex
    capacity = 3 * rows_here // group_size
    slots = group_size * capacity
    route_count = rows_here * top_count
    flat_routes = route_experts.reshape(rows_here, top_count).T.reshape(1, route_count)
    gates = route_gate.reshape(rows_here, top_count)
    named = flat_routes == jnp.arange(group_size, dtype=jnp.int32)[:, None]
    order = jnp.arange(route_count, dtype=jnp.int32)
    earlier = (order[:, None] < order[None, :]).astype(BF)
    rank = jnp.dot(named.astype(BF), earlier, preferred_element_type=F32)
    first = (jnp.arange(group_size, dtype=jnp.int32) * capacity).astype(F32)[:, None]
    slot_of = jnp.sum(jnp.where(named, rank + first, 0.0), axis=0, keepdims=True)
    place = (
        jnp.arange(slots, dtype=jnp.int32)[:, None] == slot_of.astype(jnp.int32)
    ).astype(BF)
    place_each = [place[:, k * rows_here : (k + 1) * rows_here] for k in range(top_count)]
    place_any = functools.reduce(jnp.add, place_each)
    shaped = (group_size, capacity, features)

    gated = jnp.concatenate(
        [(upstream * gates[:, k : k + 1]).astype(BF) for k in range(top_count)], axis=0
    )
    send_upstream = dot(place, gated, 1, 0).astype(BF)
    send_upstream, _ = lax.optimization_barrier((send_upstream, entry_t))
    came_upstream = lax.all_to_all(
        send_upstream.reshape(shaped), GROUP, 0, 0, tiled=True
    ).reshape(slots, features)
    ups = [came_upstream] + [
        lax.ppermute(came_upstream, "seq", ring(n_seq, m)) for m in range(1, n_seq)
    ]

    parts = lax.all_to_all(part.reshape(n_seq, rows_here, features), "seq", 0, 0, tiled=True)
    hidden = inputs + jnp.sum(parts.astype(F32), axis=0)
    scale_two = rms_scale(hidden)
    normed_two = (hidden * scale_two * gain_two).astype(BF)

    send_rows = dot(place_any, normed_two, 1, 0).astype(BF)
    came_rows = lax.all_to_all(
        send_rows.reshape(shaped), GROUP, 0, 0, tiled=True
    ).reshape(slots, features)
    rows = [came_rows] + [
        lax.ppermute(came_rows, "seq", ring(n_seq, m)) for m in range(1, n_seq)
    ]
    w_up, w_down = expert_up[0], expert_down[0]
    worked = [expert(rows[m], ups[m], w_up, w_down) for m in range(n_seq)]
    backs = [worked[0][0]] + [
        lax.ppermute(worked[m][0], "seq", back_ring(n_seq, m)) for m in range(1, n_seq)
    ]
    back_sum = functools.reduce(jnp.add, [b.astype(F32) for b in backs]).astype(BF)
    returned_back = lax.all_to_all(
        back_sum.reshape(shaped), GROUP, 0, 0, tiled=True
    ).reshape(slots, features)
    up_grad, down_grad = expert_grad(
        rows, [w[3] for w in worked], [w[2] for w in worked], ups
    )

    back_normed_two = dot(place_any, returned_back, 0, 0)
    upper_two = back_normed_two * gain_two
    gain_two_grad = jnp.sum(back_normed_two * hidden * scale_two, axis=0)
    back_hidden = upstream + scale_two * (
        upper_two
        - hidden * scale_two * scale_two * jnp.mean(upper_two * hidden, axis=1, keepdims=True)
    )
    up_hidden = spread_out(back_hidden.astype(BF), "seq").reshape(length, features)

    results = [w[1] for w in worked]
    *results, _ = lax.optimization_barrier((*results, back_sum))
    outs = [results[0]] + [
        lax.ppermute(results[m], "seq", back_ring(n_seq, m)) for m in range(1, n_seq)
    ]
    out_sum = functools.reduce(jnp.add, [o.astype(F32) for o in outs]).astype(BF)
    returned_out = lax.all_to_all(
        out_sum.reshape(shaped), GROUP, 0, 0, tiled=True
    ).reshape(slots, features)
    block_output = hidden
    for k in range(top_count):
        block_output = block_output + dot(place_each[k], returned_out, 0, 0) * gates[:, k : k + 1]

    entry_grad, exit_grad, back, diag, gain_one_grad = attend_back(
        heads, size, up_hidden, exit_t, qkv, ctx, log, docs_row, docs_col, lag,
        xhat, gain_one, entry_t,
    )
    halves = lax.all_to_all(
        entry_grad.reshape(n_ex, n_dp * owned, features), "expert", 0, 0, tiled=True
    )
    half = jnp.sum(halves.astype(F32), axis=0).astype(BF).reshape(n_dp, owned, features)
    mine = jnp.sum(lax.all_to_all(half, "dp", 0, 0, tiled=True).astype(F32), axis=0)
    pieces = pick(mine.reshape(per, chunk, features), inverse_rows(receive), me)
    came = [
        lax.ppermute(piece, ALL, tuple((b, a) for a, b in pair))
        for piece, pair in zip(pieces, pairs)
    ]
    entry_share = jnp.concatenate(pick(jnp.stack(came), inverse_rows(send), me), axis=0).T

    backs = lax.all_to_all(back.reshape(n_seq, rows_here, features), "seq", 0, 0, tiled=True)
    back_normed_one = jnp.sum(backs.astype(F32), axis=0)
    upper_one = back_normed_one * gain_one
    back_input = back_hidden + scale_one * (
        upper_one
        - inputs * scale_one * scale_one * jnp.mean(upper_one * inputs, axis=1, keepdims=True)
    )

    hot_back = bucket_hot(length - 1 - lane, buckets)
    bias_grad = jnp.dot(hot_back, diag.T, precision=HIGH)
    small = jnp.concatenate(
        [
            gain_one_grad.reshape(devices, share),
            gain_two_grad.reshape(devices, share),
            jnp.broadcast_to(bias_grad.reshape(1, buckets * heads), (devices, buckets * heads)),
        ],
        axis=1,
    )
    count = 2 * share + buckets * heads
    lines = -(-count // width)
    small = jnp.pad(small, ((0, 0), (0, lines * width - count))).reshape(devices, lines, width)
    upper = lax.reduce_precision(small, 8, 7)
    exit_send = jnp.concatenate(
        [
            exit_grad.reshape(devices, share, width),
            upper.astype(BF),
            (small - upper).astype(BF),
        ],
        axis=1,
    )
    exit_came = lax.all_to_all(exit_send, ALL, 0, 0, tiled=True).astype(F32)
    exit_came = exit_came.reshape(n_dp, n_seq, n_ex, share + 2 * lines, width)
    exit_came = jnp.sum(exit_came, axis=(0, 2))
    exit_share = exit_came[:, :share].transpose(0, 2, 1).reshape(features, share)
    small = (exit_came[:, share : share + lines] + exit_came[:, share + lines :]).reshape(
        n_seq, lines * width
    )
    gain_one_share = jnp.sum(small[:, :share], axis=0)
    gain_two_share = jnp.sum(small[:, share : 2 * share], axis=0)
    bias_total = (
        small[:, 2 * share : count]
        .reshape(n_seq, buckets, heads)
        .transpose(1, 0, 2)
        .reshape(buckets, head_count)
    )
    return (
        block_output.reshape(block_input.shape),
        back_input.reshape(block_input.shape),
        gain_one_share,
        entry_share,
        exit_share,
        bias_total,
        gain_two_share,
        up_grad[None],
        down_grad[None],
    )


def solution(mesh):
    tokens = P(("dp", "expert"), "seq", None)
    columns = P(None, ALL)
    placed = (
        tokens,
        P(("dp", "expert"), None),
        tokens,
        tokens,
        P(ALL),
        columns,
        columns,
        P(),
        P(ALL),
        P(("dp", "expert"), None, "seq"),
        P(("dp", "expert"), "seq", None),
        tokens,
    )
    return jax.shard_map(
        local,
        mesh=mesh,
        in_specs=placed,
        out_specs=(
            tokens,
            tokens,
            P(ALL),
            columns,
            columns,
            P(),
            P(ALL),
            P(("dp", "expert"), None, "seq"),
            P(("dp", "expert"), "seq", None),
        ),
        check_vma=False,
    )
```

```python
import functools
import math

import jax
import jax.numpy as jnp
import numpy as np
from jax import lax
from jax.experimental import pallas as pl
from jax.experimental.pallas import tpu as pltpu
from jax.sharding import PartitionSpec as P

EPSILON = 1e-06
SLOPE = 0.7978845608028654
CUBIC = 0.044715
LIMITS = (19, 21, 24, 27, 31, 35, 40, 46, 52, 59, 67, 77, 87, 99, 113)
MASKED = -1e30
HIGH = lax.Precision.HIGHEST
ALL = ("dp", "seq", "expert")
GROUP = ("dp", "expert")
BLOCK = 128
BF = jnp.bfloat16
F32 = jnp.float32


def dot(left, right, left_dim, right_dim):
    return lax.dot_general(
        left, right, (((left_dim,), (right_dim,)), ((), ())), preferred_element_type=F32
    )


def rms_scale(values):
    return lax.rsqrt(jnp.mean(values * values, axis=-1, keepdims=True) + EPSILON)


def bucket_hot(lag, count):
    bucket = jnp.minimum(lag, 16)
    for threshold in LIMITS:
        bucket = bucket + (lag >= threshold).astype(jnp.int32)
    return (jnp.arange(count, dtype=jnp.int32)[:, None] == bucket[None, :]).astype(F32)


@functools.lru_cache(maxsize=None)
def weight_routes(features, columns, n_dp, n_seq, n_ex):
    width = features // n_seq
    chunk = math.gcd(columns, width)
    per = columns // chunk
    devices = n_dp * n_seq * n_ex
    edges = []
    for group in range(n_seq):
        index = 0
        for part in range(3):
            for i in range(width // chunk):
                piece = (part * features + group * width) // chunk + i
                ex, rest = divmod(index, n_dp * per)
                dp, slot = divmod(rest, per)
                target = (dp * n_seq + group) * n_ex + ex
                edges.append((piece // per, piece % per, target, slot))
                index += 1
    rounds = []
    left = list(edges)
    for _ in range(per):
        out_edges = [[] for _ in range(devices)]
        for edge in left:
            out_edges[edge[0]].append(edge)
        matched = {}

        def place(source, seen):
            for edge in out_edges[source]:
                if edge[2] in seen:
                    continue
                seen.add(edge[2])
                if edge[2] not in matched or place(matched[edge[2]][0], seen):
                    matched[edge[2]] = edge
                    return True
            return False

        for source in range(devices):
            assert place(source, set())
        rounds.append(sorted(matched.values()))
        for edge in matched.values():
            left.remove(edge)
    pairs = tuple(tuple((e[0], e[2]) for e in r) for r in rounds)
    send = np.zeros((devices, per), np.int32)
    receive = np.zeros((devices, per), np.int32)
    for m, r in enumerate(rounds):
        for source, sub, target, slot in r:
            send[source, m] = sub
            receive[target, slot] = m
    return chunk, per, pairs, send, receive


def inverse_rows(table):
    return np.argsort(table, axis=1).astype(np.int32)


def positions_of(count, sign):
    me, step = np.arange(count)[:, None], np.arange(count)[None, :]
    return me ^ step if count & (count - 1) == 0 else (me + sign * step) % count


class Info:
    def __init__(self, features, columns, n_dp, n_seq, n_ex):
        self.chunk, self.per, self.pairs, send, receive = weight_routes(
            features, columns, n_dp, n_seq, n_ex
        )
        device = np.arange(n_dp * n_seq * n_ex)
        dp, seq, ex = device // (n_seq * n_ex), device // n_ex % n_seq, device % n_ex
        parts = {
            "send_sub": send,
            "slot_round": receive,
            "sub_round": inverse_rows(send),
            "send_slot": inverse_rows(receive),
            "from_seq": positions_of(n_seq, -1)[seq],
            "to_seq": positions_of(n_seq, 1)[seq],
            "from_dp": positions_of(n_dp, -1)[dp],
            "to_dp": positions_of(n_dp, 1)[dp],
            "from_ex": positions_of(n_ex, -1)[ex],
            "to_ex": positions_of(n_ex, 1)[ex],
        }
        self.start = {}
        width = 0
        for name, part in parts.items():
            self.start[name] = width
            width += part.shape[1]
        self.table = np.concatenate(list(parts.values()), axis=1).astype(np.int32)

    def at(self, ref, name, i):
        return ref[self.start[name] + i]


def chosen(values, index):
    out = values[0]
    for i in range(1, len(values)):
        out = jnp.where(index == i, values[i], out)
    return out


def specs(arrays):
    return [pl.BlockSpec(memory_space=pltpu.SMEM)] + [
        pl.BlockSpec(memory_space=pltpu.VMEM)
    ] * arrays


def small_call(kernel, info_row, arrays, outs, scratch):
    return pl.pallas_call(
        kernel,
        in_specs=specs(len(arrays)),
        out_shape=tuple(jax.ShapeDtypeStruct(shape, kind) for shape, kind in outs),
        scratch_shapes=[pltpu.VMEM(shape, kind) for shape, kind in scratch],
    )(info_row, *arrays)


def whole_tiles(rows):
    return -(-rows // 16) * 16


def pick_kernel(info, row_ref, entry_ref, *out_refs):
    entry = entry_ref[...].astype(F32)
    chunk = info.chunk
    parts = [entry[i * chunk : (i + 1) * chunk, :] for i in range(info.per)]
    for i, out_ref in enumerate(out_refs):
        out_ref[...] = chosen(parts, info.at(row_ref, "send_sub", i)).astype(BF)


def place_kernel(info, n_seq, share, row_ref, *refs):
    per, chunk = info.per, info.chunk
    came, exit_ref, gains = refs[:per], refs[per], refs[per + 1 : per + 1 + n_seq]
    out_ref, line_ref = refs[per + 1 + n_seq :]
    head = whole_tiles(share + n_seq)
    line_ref[...] = jnp.zeros_like(line_ref)
    line_ref[:share, :] = exit_ref[...].astype(F32)
    rows = [ref[...].astype(F32) for ref in gains]
    for i in range(n_seq):
        value = rows[0]
        for j in range(1, n_seq):
            value = jnp.where(info.at(row_ref, "from_seq", j) == i, rows[j], value)
        line_ref[share + i : share + i + 1, :] = value
    parts = [ref[...].astype(F32) for ref in came]
    for i in range(per):
        line_ref[head + i * chunk : head + (i + 1) * chunk, :] = chosen(
            parts, info.at(row_ref, "slot_round", i)
        )
    out_ref[...] = line_ref[...].astype(BF)


def arrange_kernel(info, n_dp, n_seq, n_ex, share, owned, row_ref, *refs):
    blocks, refs = refs[: n_dp * n_ex], refs[n_dp * n_ex :]
    entry_ref, gain_ref, *exit_refs = refs[: 2 + n_seq]
    all_ref, line_ref, exits_ref = refs[2 + n_seq :]
    width = exits_ref.shape[3]
    head = whole_tiles(share + n_seq)
    for i in range(n_dp):
        for j in range(n_ex):
            spot = info.at(row_ref, "from_ex", j) * n_dp + info.at(row_ref, "from_dp", i)
            all_ref[spot] = blocks[i * n_ex + j][...]
    for spot in range(n_ex * n_dp):
        ex, dp = divmod(spot, n_dp)
        value = all_ref[spot].astype(F32)
        line_ref[spot * owned : (spot + 1) * owned, :] = value[head : head + owned, :]
        for seq in range(n_seq):
            exits_ref[seq, spot] = value[:share, seq * width : (seq + 1) * width]
            lane = ((dp * n_seq + seq) * n_ex + ex) * share
            for k in range(2):
                gain_ref[k : k + 1, lane : lane + share] = value[
                    share + seq : share + seq + 1, k * share : (k + 1) * share
                ]
    entry_ref[...] = line_ref[...].astype(BF)
    for i in range(n_seq):
        exit_refs[i][...] = exits_ref[info.at(row_ref, "to_seq", i)].astype(BF)


def pack_kernel(info, n_dp, n_seq, n_ex, share, owned, row_ref, *refs):
    exits, refs = refs[:n_seq], refs[n_seq:]
    entry_ref, diag_ref, one_ref, two_ref, hot_ref = refs[:5]
    out_refs, (four_ref, small_ref, all_ref) = refs[5 : 5 + n_ex], refs[5 + n_ex :]
    width = exits[0].shape[2]
    heads, buckets = diag_ref.shape[0], hot_ref.shape[0]
    head = whole_tiles(share + 2)
    for i in range(n_seq):
        four_ref[info.at(row_ref, "from_seq", i)] = exits[i][...].astype(F32)
    bias = lax.dot_general(
        diag_ref[...], hot_ref[...], (((1,), (1,)), ((), ())), precision=HIGH,
        preferred_element_type=F32,
    )
    small_ref[...] = jnp.zeros_like(small_ref)
    all_ref[...] = jnp.zeros_like(all_ref)
    for seq in range(n_seq):
        for k in range(heads):
            lane = seq * width + 2 * share + k * buckets
            small_ref[0:1, lane : lane + buckets] = bias[k : k + 1, :]
    entry = entry_ref[...].astype(F32)
    for spot in range(n_ex * n_dp):
        ex, dp = divmod(spot, n_dp)
        for seq in range(n_seq):
            to = seq * width
            all_ref[ex, dp, :share, to : to + width] = four_ref[
                seq, dp, ex * share : (ex + 1) * share, :
            ]
            lane = ((dp * n_seq + seq) * n_ex + ex) * share
            small_ref[0:1, to : to + share] = one_ref[:, lane : lane + share]
            small_ref[0:1, to + share : to + 2 * share] = two_ref[:, lane : lane + share]
        small = small_ref[0:1, :]
        upper = small.astype(BF).astype(F32)
        all_ref[ex, dp, share : share + 1, :] = upper
        all_ref[ex, dp, share + 1 : share + 2, :] = small - upper
        all_ref[ex, dp, head : head + owned, :] = entry[spot * owned : (spot + 1) * owned, :]
    for i in range(n_ex):
        out_refs[i][...] = all_ref[info.at(row_ref, "to_ex", i)].astype(BF)


def fold_kernel(info, n_dp, n_ex, share, row_ref, *refs):
    parts, out_refs, all_ref = refs[:n_ex], refs[n_ex : n_ex + n_dp], refs[n_ex + n_dp]
    for dp in range(n_dp):
        total = parts[0][dp].astype(F32)
        for part in parts[1:]:
            total = total + part[dp].astype(F32)
        all_ref[dp] = total
        small = total[share : share + 1, :] + total[share + 1 : share + 2, :]
        upper = small.astype(BF).astype(F32)
        all_ref[dp, share : share + 1, :] = upper
        all_ref[dp, share + 1 : share + 2, :] = small - upper
    for i in range(n_dp):
        out_refs[i][...] = all_ref[info.at(row_ref, "to_dp", i)].astype(BF)


def finish_kernel(info, n_dp, n_seq, share, row_ref, *refs):
    parts, refs = refs[:n_dp], refs[n_dp:]
    exit_ref, *refs = refs
    piece_refs, small_refs, four_ref = refs[: info.per], refs[info.per : -1], refs[-1]
    head, chunk = whole_tiles(share + 2), info.chunk
    total = parts[0][...].astype(F32)
    for part in parts[1:]:
        total = total + part[...].astype(F32)
    exit_ref[...] = total[:share, :]
    small = total[share : share + 1, :] + total[share + 1 : share + 2, :]
    width = four_ref.shape[2]
    for seq in range(n_seq):
        four_ref[seq] = small[:, seq * width : (seq + 1) * width]
    for i in range(n_seq):
        small_refs[i][...] = four_ref[info.at(row_ref, "to_seq", i)]
    pieces = [total[head + i * chunk : head + (i + 1) * chunk, :] for i in range(info.per)]
    for i in range(info.per):
        piece_refs[i][...] = chosen(pieces, info.at(row_ref, "send_slot", i))


def close_kernel(info, n_seq, share, heads, row_ref, *refs):
    came, small, refs = refs[: info.per], refs[info.per : info.per + n_seq], refs[info.per + n_seq :]
    entry_ref, gain_ref, bias_ref, four_ref = refs
    chunk, buckets = info.chunk, bias_ref.shape[1]
    parts = [ref[...] for ref in came]
    for i in range(info.per):
        entry_ref[i * chunk : (i + 1) * chunk, :] = chosen(parts, info.at(row_ref, "sub_round", i))
    for i in range(n_seq):
        four_ref[info.at(row_ref, "from_seq", i)] = small[i][...]
    total = four_ref[0]
    for seq in range(1, n_seq):
        total = total + four_ref[seq]
    gain_ref[0:1, :] = total[:, :share]
    gain_ref[1:2, :] = total[:, share : 2 * share]
    for seq in range(n_seq):
        for k in range(heads):
            lane = 2 * share + k * buckets
            bias_ref[seq * heads + k : seq * heads + k + 1, :] = four_ref[
                seq, :, lane : lane + buckets
            ]


def allowed_of(docs_row, docs_col, start, rows, keys):
    query = start + lax.broadcasted_iota(jnp.int32, (rows, keys), 0)
    key = lax.broadcasted_iota(jnp.int32, (rows, keys), 1)
    return (key <= query) & (docs_col[start : start + rows, :] == docs_row[:, :keys])


def bias_rows(lag_ref, head, start, rows, keys):
    length = lag_ref.shape[1]
    flat = jnp.broadcast_to(lag_ref[head : head + 1, :], (rows, length))
    return pltpu.roll(flat, start, 1, stride=1, stride_axis=0)[:, :keys]


def aligned(block, index):
    return pl.ds(pl.multiple_of(index * block, block), block)


def attend_kernel(info, heads, size, count, row_ref, *refs):
    x_refs, refs = refs[:count], refs[count:]
    gain_ref, w_ref, doc_ref, col_ref, lag_ref, x_ref, qkv_ref, ctx_ref, log_ref = refs
    length = x_ref.shape[0]
    rows = length // count
    width = heads * size
    factor = size ** (-0.5)
    for i in range(count):
        x_ref[aligned(rows, info.at(row_ref, "from_seq", i)), :] = x_refs[i][...]
    normed = (x_ref[...].astype(F32) * gain_ref[0:1, :]).astype(BF)
    qkv_ref[...] = dot(normed, w_ref[...], 1, 1).astype(BF)
    for start in range(0, length, BLOCK):
        keys = start + BLOCK
        allowed = allowed_of(doc_ref, col_ref, start, BLOCK, keys)
        for head in range(heads):
            lo = head * size
            q = qkv_ref[start:keys, lo : lo + size]
            k = qkv_ref[:keys, width + lo : width + lo + size]
            v = qkv_ref[:keys, 2 * width + lo : 2 * width + lo + size]
            scores = dot(q, k, 1, 1) * factor + bias_rows(lag_ref, head, start, BLOCK, keys)
            scores = jnp.where(allowed, scores, MASKED)
            peak = jnp.max(scores, axis=1, keepdims=True)
            raised = jnp.exp(scores - peak)
            total = jnp.sum(raised, axis=1, keepdims=True)
            weights = (raised / total).astype(BF)
            log_ref[start:keys, head : head + 1] = peak + jnp.log(total)
            ctx_ref[start:keys, lo : lo + size] = dot(weights, v, 1, 0).astype(BF)


def attend(info, heads, size, info_row, blocks, gain, w, docs_row, docs_col, lag):
    count = len(blocks)
    rows, features = blocks[0].shape
    length = rows * count
    width = heads * size
    return small_call(
        functools.partial(attend_kernel, info, heads, size, count),
        info_row,
        (*blocks, gain, w, docs_row, docs_col, lag),
        [
            ((length, features), BF),
            ((length, 3 * width), BF),
            ((length, width), BF),
            ((length, heads), F32),
        ],
        [],
    )


def leave_kernel(info, n_dp, n_seq, n_ex, row_ref, ctx_ref, *refs):
    exits, refs = refs[:n_seq], refs[n_seq:]
    exit_ref, part_refs, (four_ref, line_ref) = refs[0], refs[1 : 1 + n_seq], refs[1 + n_seq :]
    rows = part_refs[0].shape[0]
    share = exits[0].shape[1]
    for i in range(n_seq):
        four_ref[info.at(row_ref, "from_seq", i)] = exits[i][...].astype(F32)
    for dp in range(n_dp):
        for seq in range(n_seq):
            for ex in range(n_ex):
                start = ((dp * n_seq + seq) * n_ex + ex) * share
                line_ref[start : start + share, :] = four_ref[seq, ex * n_dp + dp]
    exit_ref[...] = line_ref[...].astype(BF)
    for i, part_ref in enumerate(part_refs):
        block = aligned(rows, info.at(row_ref, "to_seq", i))
        part_ref[...] = dot(ctx_ref[block, :], exit_ref[...], 1, 1).astype(BF)


def leave(info, n_dp, n_seq, n_ex, info_row, ctx, exits):
    spots, share, width = exits[0].shape
    features = spots * share * n_seq
    out = small_call(
        functools.partial(leave_kernel, info, n_dp, n_seq, n_ex),
        info_row,
        (ctx, *exits),
        [((features, width), BF)] + [((ctx.shape[0] // n_seq, features), BF)] * n_seq,
        [((n_seq, spots, share, width), F32), ((features, width), F32)],
    )
    return out[0], out[1:]


def leave_back_kernel(info, count, n_dp, share, row_ref, *refs):
    up_refs, refs = refs[:count], refs[count:]
    ctx_ref, up_ref, *grad_refs, all_ref = refs
    rows = up_refs[0].shape[0]
    for i in range(count):
        up_ref[aligned(rows, info.at(row_ref, "from_seq", i)), :] = up_refs[i][...]
    grad = dot(up_ref[...], ctx_ref[...], 0, 0)
    for dp in range(n_dp):
        for i in range(count):
            start = (dp * count + i) * share
            all_ref[i, dp] = grad[start : start + share, :]
    for i in range(count):
        grad_refs[i][...] = all_ref[info.at(row_ref, "to_seq", i)].astype(BF)


def leave_back(info, n_dp, info_row, blocks, ctx):
    count = len(blocks)
    rows, features = blocks[0].shape
    share = features // (n_dp * count)
    width = ctx.shape[1]
    return small_call(
        functools.partial(leave_back_kernel, info, count, n_dp, share),
        info_row,
        (*blocks, ctx),
        [((rows * count, features), BF)] + [((n_dp, share, width), BF)] * count,
        [((count, n_dp, share, width), F32)],
    )


def attend_back_kernel(info, heads, size, count, row_ref, *refs):
    up_ref, exit_ref, qkv_ref, log_ref, doc_ref, col_ref, lag_ref, x_ref, gain_ref, w_ref = refs[:10]
    diag_ref, gain_grad_ref, entry_ref, *refs = refs[10:]
    back_refs, (bctx_ref, bqkv_ref, bk_ref, bv_ref, lines_ref) = refs[:count], refs[count:]
    length = up_ref.shape[0]
    rows = length // count
    width = heads * size
    factor = size ** (-0.5)
    bctx_ref[...] = dot(up_ref[...], exit_ref[...], 1, 0).astype(BF)
    bk_ref[...] = jnp.zeros_like(bk_ref)
    bv_ref[...] = jnp.zeros_like(bv_ref)
    lines_ref[...] = jnp.zeros_like(lines_ref)
    for start in range(0, length, BLOCK):
        keys = start + BLOCK
        allowed = allowed_of(doc_ref, col_ref, start, BLOCK, keys)
        for head in range(heads):
            lo = head * size
            q = qkv_ref[start:keys, lo : lo + size]
            k = qkv_ref[:keys, width + lo : width + lo + size]
            v = qkv_ref[:keys, 2 * width + lo : 2 * width + lo + size]
            bc = bctx_ref[start:keys, lo : lo + size]
            scores = dot(q, k, 1, 1) * factor + bias_rows(lag_ref, head, start, BLOCK, keys)
            probs = jnp.where(
                allowed, jnp.exp(scores - log_ref[start:keys, head : head + 1]), 0.0
            )
            back_probs = dot(bc, v, 1, 1)
            row_dot = jnp.sum(probs * back_probs, axis=1, keepdims=True)
            back_scores = probs * (back_probs - row_dot)
            scaled = (back_scores * factor).astype(BF)
            bqkv_ref[start:keys, lo : lo + size] = dot(scaled, k, 1, 0).astype(BF)
            bk_ref[:keys, lo : lo + size] += dot(scaled, q, 0, 0)
            bv_ref[:keys, lo : lo + size] += dot(probs.astype(BF), bc, 0, 0)
            lined = jnp.zeros((8, keys), F32)
            for row in range(0, BLOCK, 8):
                lined = lined + pltpu.roll(
                    back_scores[row : row + 8, :], (keys - start - row - 8) % keys, 1
                )
            lines_ref[8 * head : 8 * head + 8, length - keys :] += lined
    for head in range(heads):
        total = jnp.zeros((1, length), F32)
        for row in range(8):
            total = total + pltpu.roll(
                lines_ref[8 * head + row : 8 * head + row + 1, :], 7 - row, 1
            )
        diag_ref[head : head + 1, :] = total
    bqkv_ref[:, width : 2 * width] = bk_ref[...].astype(BF)
    bqkv_ref[:, 2 * width :] = bv_ref[...].astype(BF)
    normed = (x_ref[...].astype(F32) * gain_ref[0:1, :]).astype(BF)
    entry_ref[...] = dot(bqkv_ref[...], normed, 0, 0).astype(BF)
    gain_grad = jnp.zeros(gain_grad_ref.shape, F32)
    for i in range(count):
        block = aligned(rows, info.at(row_ref, "to_seq", i))
        back = dot(bqkv_ref[block, :], w_ref[...], 1, 0)
        back_refs[i][...] = back.astype(BF)
        gain_grad += jnp.sum(back * x_ref[block, :].astype(F32), axis=0, keepdims=True)
    gain_grad_ref[...] = gain_grad


def attend_back(
    info, heads, size, count, info_row, up, exit_t, qkv, log, docs_row, docs_col, lag, x, gain, w
):
    length, features = up.shape
    width = heads * size
    diag, gain_grad, entry, *backs = small_call(
        functools.partial(attend_back_kernel, info, heads, size, count),
        info_row,
        (up, exit_t, qkv, log, docs_row, docs_col, lag, x, gain, w),
        [
            ((heads, length), F32),
            ((1, features), F32),
            ((3 * width, features), BF),
            *[((length // count, features), BF)] * count,
        ],
        [
            ((length, width), BF),
            ((length, 3 * width), BF),
            ((length, width), F32),
            ((length, width), F32),
            ((8 * heads, length), F32),
        ],
    )
    return diag, gain_grad, entry, backs


def expert_kernel(count, rows_ref, up_ref, *refs):
    w_ups, w_downs, refs = refs[:count], refs[count : 2 * count], refs[2 * count :]
    back_ref, result_ref, acts, bbs = refs[0], refs[1], refs[2 : 2 + count], refs[2 + count :]
    for i in range(count):
        before = dot(rows_ref[...], w_ups[i][...], 1, 0)
        tangent = jnp.tanh(SLOPE * (before + CUBIC * before * before * before))
        acts[i][...] = (0.5 * before * (1.0 + tangent)).astype(BF)
        slope = 0.5 * (1.0 + tangent) + 0.5 * before * (1.0 - tangent * tangent) * SLOPE * (
            1.0 + 3.0 * CUBIC * before * before
        )
        bbs[i][...] = (dot(up_ref[...], w_downs[i][...], 1, 1) * slope).astype(BF)
    back = dot(bbs[0][...], w_ups[0][...], 1, 1)
    for i in range(1, count):
        back = back + dot(bbs[i][...], w_ups[i][...], 1, 1)
    back_ref[...] = back.astype(BF)
    result = dot(acts[0][...], w_downs[0][...], 1, 0)
    for i in range(1, count):
        result = result + dot(acts[i][...], w_downs[i][...], 1, 0)
    result_ref[...] = result.astype(BF)


def expert(rows, upstream, w_ups, w_downs):
    count = len(w_ups)
    tokens, features = rows.shape
    hidden = w_ups[0].shape[1]
    out = pl.pallas_call(
        functools.partial(expert_kernel, count),
        out_shape=(
            *[jax.ShapeDtypeStruct((tokens, features), BF)] * 2,
            *[jax.ShapeDtypeStruct((tokens, hidden), BF)] * (2 * count),
        ),
        name="expert",
    )(rows, upstream, *w_ups, *w_downs)
    return out[0], out[1], out[2 : 2 + count], out[2 + count :]


def expert_grad_kernel(count, *refs):
    rows, bbs = refs[:count], refs[count : 2 * count]
    acts, ups = refs[2 * count : 3 * count], refs[3 * count : 4 * count]
    up_ref, down_ref = refs[4 * count :]
    total = dot(rows[0][...], bbs[0][...], 0, 0)
    for i in range(1, count):
        total = total + dot(rows[i][...], bbs[i][...], 0, 0)
    up_ref[...] = total.astype(up_ref.dtype)
    total = dot(acts[0][...], ups[0][...], 0, 0)
    for i in range(1, count):
        total = total + dot(acts[i][...], ups[i][...], 0, 0)
    down_ref[...] = total.astype(down_ref.dtype)


def expert_grad(rows, bbs, acts, ups, kind):
    features, hidden = rows[0].shape[1], bbs[0].shape[1]
    return pl.pallas_call(
        functools.partial(expert_grad_kernel, len(rows)),
        out_shape=(
            jax.ShapeDtypeStruct((features, hidden), kind),
            jax.ShapeDtypeStruct((hidden, features), kind),
        ),
        name="expert_grad",
    )(*rows, *bbs, *acts, *ups)


def target(count, me, step):
    return me ^ step if count & (count - 1) == 0 else (me + step) % count


def source(count, me, step):
    return me ^ step if count & (count - 1) == 0 else (me - step) % count


def shift(array, axis, step):
    count = lax.axis_size(axis)
    return lax.ppermute(array, axis, tuple((i, target(count, i, step)) for i in range(count)))


def gathered(array, axis, steps):
    return [array] + [shift(array, axis, step) for step in steps]


def exchanged(array, axis):
    return lax.all_to_all(array, axis, 0, 0, tiled=True)


def traded(blocks, axis, steps):
    return [blocks[0]] + [shift(block, axis, step) for block, step in zip(blocks[1:], steps)]


def summed(blocks, axis, steps):
    came = traded(blocks, axis, steps)
    return functools.reduce(jnp.add, [block.astype(F32) for block in came])


def handed_back(blocks, axis, steps):
    count = lax.axis_size(axis)
    return summed(blocks, axis, tuple(source(count, 0, step) for step in steps))


def after(arrays, *others):
    return lax.optimization_barrier((tuple(arrays), others))[0]


def local(
    block_input,
    documents,
    route_experts,
    route_gate,
    first_gain,
    entry_weight,
    exit_weight,
    position_bias,
    second_gain,
    expert_up,
    expert_down,
    cotangent,
):
    n_dp, n_seq, n_ex = (lax.axis_size(name) for name in ALL)
    group_count = n_dp * n_ex
    rows_here, features = block_input.shape[1:]
    buckets, head_count = position_bias.shape
    size = features // head_count
    heads = head_count // n_seq
    width = heads * size
    top_count = route_experts.shape[2]
    length = rows_here * n_seq
    me = lax.axis_index(ALL)
    here = lax.axis_index("seq")
    inputs = block_input.reshape(rows_here, features)
    upstream = cotangent.reshape(rows_here, features)

    seq_steps = tuple(range(1, n_seq))
    owned = entry_weight.shape[1]
    share = exit_weight.shape[1]
    info = Info(features, owned, n_dp, n_seq, n_ex)
    per, chunk = info.per, info.chunk
    info_row = lax.dynamic_slice(jnp.asarray(info.table), (me, 0), (1, info.table.shape[1]))
    info_row = info_row.reshape(info.table.shape[1])

    pieces = small_call(
        functools.partial(pick_kernel, info),
        info_row, (entry_weight.T,), [((chunk, features), BF)] * per, [],
    )
    came = [lax.ppermute(piece, ALL, pair) for piece, pair in zip(pieces, info.pairs)]
    gains = jnp.pad(jnp.concatenate([first_gain, second_gain]), (0, features - 2 * share))
    gain_rows = gathered(gains[None], "seq", seq_steps)
    scale_one = rms_scale(inputs)
    xhats = gathered((inputs * scale_one).astype(BF), "seq", seq_steps)
    padded = whole_tiles(share + n_seq) + whole_tiles(owned)
    (weights,) = small_call(
        functools.partial(place_kernel, info, n_seq, share),
        info_row, (*came, exit_weight.T, *gain_rows),
        [((padded, features), BF)], [((padded, features), F32)],
    )
    weights = gathered(weights, "dp", range(1, n_dp))
    weights = [block for weight in weights for block in gathered(weight, "expert", range(1, n_ex))]
    entry_t, gains, *exits = small_call(
        functools.partial(arrange_kernel, info, n_dp, n_seq, n_ex, share, owned),
        info_row, weights,
        [((3 * width, features), BF), ((2, features), F32)]
        + [((group_count, share, width), BF)] * n_seq,
        [
            ((group_count, padded, features), BF),
            ((3 * width, features), F32),
            ((n_seq, group_count, share, width), F32),
        ],
    )
    gain_one, gain_two = gains[0:1], gains[1:2]
    exits = exits[:1] + [shift(part, "seq", step) for part, step in zip(exits[1:], seq_steps)]

    inner = 2 if n_seq > 1 and n_seq & (n_seq - 1) == 0 else 1
    in_steps = tuple(range(1, inner))
    out_steps = tuple(range(inner, n_seq, inner))
    w_send = (expert_up[0], expert_down[0])
    w_ups = gathered(w_send[0], "seq", out_steps)
    w_downs = gathered(w_send[1], "seq", out_steps)

    group_size = n_dp * n_ex
    capacity = 3 * rows_here // group_size
    slots = group_size * capacity
    route_count = rows_here * top_count
    flat_routes = route_experts.reshape(rows_here, top_count).T.reshape(1, route_count)
    gates = route_gate.reshape(rows_here, top_count)
    named = flat_routes == jnp.arange(group_size, dtype=jnp.int32)[:, None]
    order = jnp.arange(route_count, dtype=jnp.int32)
    earlier = (order[:, None] < order[None, :]).astype(BF)
    rank = jnp.dot(named.astype(BF), earlier, preferred_element_type=F32)
    first = (jnp.arange(group_size, dtype=jnp.int32) * capacity).astype(F32)[:, None]
    slot_of = jnp.sum(jnp.where(named, rank + first, 0.0), axis=0, keepdims=True)
    place = (
        jnp.arange(slots, dtype=jnp.int32)[:, None] == slot_of.astype(jnp.int32)
    ).astype(BF)
    place_each = [place[:, k * rows_here : (k + 1) * rows_here] for k in range(top_count)]
    place_any = functools.reduce(jnp.add, place_each)
    shaped = (group_size, capacity, features)

    gated = jnp.concatenate(
        [(upstream * gates[:, k : k + 1]).astype(BF) for k in range(top_count)], axis=0
    )
    send_upstream = dot(place, gated, 1, 0).astype(BF)
    came_upstream = exchanged(send_upstream.reshape(shaped), GROUP).reshape(slots, features)

    docs = documents.reshape(length)
    docs_row, docs_col = docs.reshape(1, length), docs.reshape(length, 1)
    lane = jnp.arange(length, dtype=jnp.int32)
    hot = bucket_hot(jnp.where(lane == 0, 0, length - lane), buckets)
    bias_here = lax.dynamic_slice_in_dim(position_bias.T, here * heads, heads)
    lag = jnp.dot(bias_here, hot, precision=HIGH)
    hot_back = bucket_hot(length - 1 - lane, buckets)
    (lag,) = after((lag,), send_upstream)
    xfull, qkv, ctx, log = attend(
        info, heads, size, info_row, xhats, gains, entry_t, docs_row, docs_col, lag
    )
    exit_t, parts = leave(info, n_dp, n_seq, n_ex, info_row, ctx, exits)

    hidden = inputs + summed(parts, "seq", seq_steps)
    scale_two = rms_scale(hidden)
    normed_two = (hidden * scale_two * gain_two).astype(BF)

    send_rows = dot(place_any, normed_two, 1, 0).astype(BF)
    ups = gathered(came_upstream, "seq", in_steps)
    came_rows = exchanged(send_rows.reshape(shaped), GROUP).reshape(slots, features)
    rows = gathered(came_rows, "seq", in_steps)
    worked = []
    for m in range(inner):
        worked.append(expert(rows[m], ups[m], w_ups, w_downs))
    back_sum = handed_back([w[0] for w in worked], "seq", in_steps).astype(BF)
    returned_back = exchanged(back_sum.reshape(shaped), GROUP).reshape(slots, features)
    grads = []
    for j in range(n_seq // inner):
        bbs, acts = [w[3][j] for w in worked], [w[2][j] for w in worked]
        grads.append(expert_grad(rows, bbs, acts, ups, BF if j else F32))
    back_normed_two = dot(place_any, returned_back, 0, 0)
    upper_two = back_normed_two * gain_two
    gain_two_grad = jnp.sum(back_normed_two * hidden * scale_two, axis=0, keepdims=True)
    back_hidden = upstream + scale_two * (
        upper_two
        - hidden * scale_two * scale_two * jnp.mean(upper_two * hidden, axis=1, keepdims=True)
    )
    up_hiddens = gathered(back_hidden.astype(BF), "seq", seq_steps)

    results = [w[1] for w in worked]
    out_sum = handed_back(results, "seq", in_steps).astype(BF)
    returned_out = exchanged(out_sum.reshape(shaped), GROUP).reshape(slots, features)
    block_output = hidden
    for k in range(top_count):
        block_output = block_output + dot(place_each[k], returned_out, 0, 0) * gates[:, k : k + 1]

    up_full, *exit_grads = leave_back(info, n_dp, info_row, up_hiddens, ctx)
    exit_grads = exit_grads[:1] + [
        shift(part, "seq", step)
        for part, step in zip(exit_grads[1:], seq_steps)
    ]
    diag, gain_one_grad, entry_grad, backs = attend_back(
        info, heads, size, n_seq, info_row, up_full, exit_t, qkv, log, docs_row, docs_col, lag,
        xfull, gains, entry_t,
    )

    count = 2 * share + buckets * heads
    assert count <= width
    padded = whole_tiles(share + 2) + whole_tiles(owned)
    halves = small_call(
        functools.partial(pack_kernel, info, n_dp, n_seq, n_ex, share, owned),
        info_row,
        (*exit_grads, entry_grad, diag, gain_one_grad, gain_two_grad, hot_back),
        [((n_dp, padded, features), BF)] * n_ex,
        [
            ((n_seq, n_dp, n_ex * share, width), F32),
            ((8, features), F32),
            ((n_ex, n_dp, padded, features), F32),
        ],
    )
    halves = traded(halves, "expert", range(1, n_ex))
    quarters = small_call(
        functools.partial(fold_kernel, info, n_dp, n_ex, share),
        info_row, halves, [((padded, features), BF)] * n_dp,
        [((n_dp, padded, features), F32)],
    )
    quarters = traded(quarters, "dp", range(1, n_dp))
    exit_share, *rest = small_call(
        functools.partial(finish_kernel, info, n_dp, n_seq, share),
        info_row, quarters,
        [((share, features), F32)]
        + [((chunk, features), F32)] * per
        + [((1, width), F32)] * n_seq,
        [((n_seq, 1, width), F32)],
    )
    pieces, small = rest[:per], rest[per:]
    came = [
        lax.ppermute(piece, ALL, tuple((b, a) for a, b in pair))
        for piece, pair in zip(pieces, info.pairs)
    ]
    small = traded(small, "seq", seq_steps)
    entry_share, gain_shares, bias_total = small_call(
        functools.partial(close_kernel, info, n_seq, share, heads),
        info_row, (*came, *small),
        [((owned, features), F32), ((2, share), F32), ((head_count, buckets), F32)],
        [((n_seq, 1, width), F32)],
    )
    entry_share, exit_share, bias_total = entry_share.T, exit_share.T, bias_total.T
    gain_one_share, gain_two_share = gain_shares[0], gain_shares[1]

    back_normed_one = summed(backs, "seq", seq_steps)
    upper_one = back_normed_one * gain_one
    back_input = back_hidden + scale_one * (
        upper_one
        - inputs * scale_one * scale_one * jnp.mean(upper_one * inputs, axis=1, keepdims=True)
    )

    (own_up, own_down), *others = grads
    own_up, own_down = after((own_up, own_down), gain_one_grad)
    grads = [(own_up, own_down), *others]
    up_grad = handed_back([g[0] for g in grads], "seq", out_steps)
    down_grad = handed_back([g[1] for g in grads], "seq", out_steps)

    return (
        block_output.reshape(block_input.shape),
        back_input.reshape(block_input.shape),
        gain_one_share,
        entry_share,
        exit_share,
        bias_total,
        gain_two_share,
        up_grad[None],
        down_grad[None],
    )


def solution(mesh):
    tokens = P(("dp", "expert"), "seq", None)
    columns = P(None, ALL)
    placed = (
        tokens,
        P(("dp", "expert"), None),
        tokens,
        tokens,
        P(ALL),
        columns,
        columns,
        P(),
        P(ALL),
        P(("dp", "expert"), None, "seq"),
        P(("dp", "expert"), "seq", None),
        tokens,
    )

    return jax.shard_map(
        local,
        mesh=mesh,
        in_specs=placed,
        out_specs=(
            tokens,
            tokens,
            P(ALL),
            columns,
            columns,
            P(),
            P(ALL),
            P(("dp", "expert"), None, "seq"),
            P(("dp", "expert"), "seq", None),
        ),
        check_vma=False,
    )
```

```python
import functools
import math

import jax
import jax.numpy as jnp
import numpy as np
from jax import lax
from jax.experimental import pallas as pl
from jax.experimental.pallas import tpu as pltpu
from jax.sharding import PartitionSpec as P

EPSILON = 1e-06
SLOPE = 0.7978845608028654
CUBIC = 0.044715
LIMITS = (19, 21, 24, 27, 31, 35, 40, 46, 52, 59, 67, 77, 87, 99, 113)
MASKED = -1e30
HIGH = lax.Precision.HIGHEST
ALL = ("dp", "seq", "expert")
GROUP = ("dp", "expert")
BLOCK = 128
BF = jnp.bfloat16
F32 = jnp.float32


def dot(left, right, left_dim, right_dim):
    return lax.dot_general(
        left, right, (((left_dim,), (right_dim,)), ((), ())), preferred_element_type=F32
    )


def rms_scale(values):
    return lax.rsqrt(jnp.mean(values * values, axis=-1, keepdims=True) + EPSILON)


def bucket_hot(lag, count):
    bucket = jnp.minimum(lag, 16)
    for threshold in LIMITS:
        bucket = bucket + (lag >= threshold).astype(jnp.int32)
    return (jnp.arange(count, dtype=jnp.int32)[:, None] == bucket[None, :]).astype(F32)


@functools.lru_cache(maxsize=None)
def weight_routes(features, columns, n_dp, n_seq, n_ex):
    width = features // n_seq
    chunk = math.gcd(columns, width)
    per = columns // chunk
    devices = n_dp * n_seq * n_ex
    edges = []
    for group in range(n_seq):
        index = 0
        for part in range(3):
            for i in range(width // chunk):
                piece = (part * features + group * width) // chunk + i
                ex, rest = divmod(index, n_dp * per)
                dp, slot = divmod(rest, per)
                target = (dp * n_seq + group) * n_ex + ex
                edges.append((piece // per, piece % per, target, slot))
                index += 1
    rounds = []
    left = list(edges)
    for _ in range(per):
        out_edges = [[] for _ in range(devices)]
        for edge in left:
            out_edges[edge[0]].append(edge)
        matched = {}

        def place(source, seen):
            for edge in out_edges[source]:
                if edge[2] in seen:
                    continue
                seen.add(edge[2])
                if edge[2] not in matched or place(matched[edge[2]][0], seen):
                    matched[edge[2]] = edge
                    return True
            return False

        for source in range(devices):
            assert place(source, set())
        rounds.append(sorted(matched.values()))
        for edge in matched.values():
            left.remove(edge)
    pairs = tuple(tuple((e[0], e[2]) for e in r) for r in rounds)
    send = np.zeros((devices, per), np.int32)
    receive = np.zeros((devices, per), np.int32)
    for m, r in enumerate(rounds):
        for source, sub, target, slot in r:
            send[source, m] = sub
            receive[target, slot] = m
    return chunk, per, pairs, send, receive


def inverse_rows(table):
    return np.argsort(table, axis=1).astype(np.int32)


def positions_of(count, sign):
    me, step = np.arange(count)[:, None], np.arange(count)[None, :]
    return me ^ step if count & (count - 1) == 0 else (me + sign * step) % count


class Info:
    def __init__(self, features, columns, n_dp, n_seq, n_ex):
        self.chunk, self.per, self.pairs, send, receive = weight_routes(
            features, columns, n_dp, n_seq, n_ex
        )
        device = np.arange(n_dp * n_seq * n_ex)
        dp, seq, ex = device // (n_seq * n_ex), device // n_ex % n_seq, device % n_ex
        self.width = 0
        self.columns = []
        self.send_sub = self.add(send)
        self.slot_round = self.add(receive)
        self.sub_round = self.add(inverse_rows(send))
        self.send_slot = self.add(inverse_rows(receive))
        self.from_seq = self.add(positions_of(n_seq, -1)[seq])
        self.to_seq = self.add(positions_of(n_seq, 1)[seq])
        self.from_dp = self.add(positions_of(n_dp, -1)[dp])
        self.to_dp = self.add(positions_of(n_dp, 1)[dp])
        self.from_ex = self.add(positions_of(n_ex, -1)[ex])
        self.to_ex = self.add(positions_of(n_ex, 1)[ex])
        self.table = np.concatenate(self.columns, axis=1).astype(np.int32)

    def add(self, part):
        self.columns.append(part)
        self.width += part.shape[1]
        return self.width - part.shape[1]


def chosen(values, index):
    out = values[0]
    for i in range(1, len(values)):
        out = jnp.where(index == i, values[i], out)
    return out


def specs(arrays):
    return [pl.BlockSpec(memory_space=pltpu.SMEM)] + [
        pl.BlockSpec(memory_space=pltpu.VMEM)
    ] * arrays


def small_call(kernel, info_row, arrays, outs, scratch):
    return pl.pallas_call(
        kernel,
        in_specs=specs(len(arrays)),
        out_shape=tuple(jax.ShapeDtypeStruct(shape, kind) for shape, kind in outs),
        scratch_shapes=[pltpu.VMEM(shape, kind) for shape, kind in scratch],
    )(info_row, *arrays)


def whole_tiles(rows, tile=16):
    return -(-rows // tile) * tile


def pick_kernel(info, row_ref, entry_ref, *out_refs):
    entry = entry_ref[...].astype(F32)
    chunk = info.chunk
    parts = [entry[i * chunk : (i + 1) * chunk, :] for i in range(info.per)]
    for i, out_ref in enumerate(out_refs):
        out_ref[...] = chosen(parts, row_ref[info.send_sub + i]).astype(BF)


def place_kernel(info, n_seq, share, row_ref, *refs):
    per, chunk = info.per, info.chunk
    came, exit_ref, gains = refs[:per], refs[per], refs[per + 1 : per + 1 + n_seq]
    out_ref, line_ref = refs[per + 1 + n_seq :]
    head = whole_tiles(share + n_seq)
    line_ref[...] = jnp.zeros_like(line_ref)
    line_ref[:share, :] = exit_ref[...].astype(F32)
    rows = [ref[...].astype(F32) for ref in gains]
    for i in range(n_seq):
        value = rows[0]
        for j in range(1, n_seq):
            value = jnp.where(row_ref[info.from_seq + j] == i, rows[j], value)
        line_ref[share + i : share + i + 1, :] = value
    parts = [ref[...].astype(F32) for ref in came]
    for i in range(per):
        line_ref[head + i * chunk : head + (i + 1) * chunk, :] = chosen(
            parts, row_ref[info.slot_round + i]
        )
    out_ref[...] = line_ref[...].astype(BF)


def arrange_kernel(info, n_dp, n_seq, n_ex, share, owned, row_ref, *refs):
    blocks, refs = refs[: n_dp * n_ex], refs[n_dp * n_ex :]
    entry_ref, gain_ref, *exit_refs = refs[: 2 + n_seq]
    all_ref, line_ref, exits_ref = refs[2 + n_seq :]
    width = exits_ref.shape[3]
    head = whole_tiles(share + n_seq)
    for i in range(n_dp):
        for j in range(n_ex):
            spot = row_ref[info.from_ex + j] * n_dp + row_ref[info.from_dp + i]
            all_ref[spot] = blocks[i * n_ex + j][...]
    for spot in range(n_ex * n_dp):
        ex, dp = divmod(spot, n_dp)
        value = all_ref[spot].astype(F32)
        line_ref[spot * owned : (spot + 1) * owned, :] = value[head : head + owned, :]
        for seq in range(n_seq):
            exits_ref[seq, spot] = value[:share, seq * width : (seq + 1) * width]
            lane = ((dp * n_seq + seq) * n_ex + ex) * share
            for k in range(2):
                gain_ref[k : k + 1, lane : lane + share] = value[
                    share + seq : share + seq + 1, k * share : (k + 1) * share
                ]
    entry_ref[...] = line_ref[...].astype(BF)
    for i in range(n_seq):
        exit_refs[i][...] = exits_ref[row_ref[info.to_seq + i]].astype(BF)


def pack_kernel(info, n_dp, n_seq, n_ex, share, owned, row_ref, *refs):
    exits, refs = refs[:n_seq], refs[n_seq:]
    entry_ref, out_refs, (four_ref, all_ref) = refs[0], refs[1 : 1 + n_ex], refs[1 + n_ex :]
    width = exits[0].shape[2]
    head = whole_tiles(share + 2)
    for i in range(n_seq):
        four_ref[row_ref[info.from_seq + i]] = exits[i][...].astype(F32)
    all_ref[...] = jnp.zeros_like(all_ref)
    entry = entry_ref[...].astype(F32)
    for spot in range(n_ex * n_dp):
        ex, dp = divmod(spot, n_dp)
        for seq in range(n_seq):
            to = seq * width
            all_ref[ex, dp, :share, to : to + width] = four_ref[
                seq, dp, ex * share : (ex + 1) * share, :
            ]
        all_ref[ex, dp, head : head + owned, :] = entry[spot * owned : (spot + 1) * owned, :]
    for i in range(n_ex):
        out_refs[i][...] = all_ref[row_ref[info.to_ex + i]].astype(BF)


def small_kernel(info, n_dp, n_seq, n_ex, share, heads, buckets, row_ref, *refs):
    small, out_refs, (four_ref, all_ref) = refs[:n_seq], refs[n_seq:-2], refs[-2:]
    for i in range(n_seq):
        four_ref[row_ref[info.from_seq + i]] = small[i][...]
    total = four_ref[0]
    for seq in range(1, n_seq):
        total = total + four_ref[seq]
    all_ref[...] = jnp.zeros_like(all_ref)
    part = heads * buckets
    for ex in range(n_ex):
        lines = slice(ex * n_dp, (ex + 1) * n_dp)
        all_ref[ex, :, : 2 * share] = total[lines, : 2 * share]
        for seq in range(n_seq):
            lane = 2 * share + seq * part
            all_ref[ex, :, lane : lane + part] = four_ref[seq, lines, 2 * share : 2 * share + part]
    for i in range(n_ex):
        out_refs[i][...] = all_ref[row_ref[info.to_ex + i]]


def fold_kernel(info, n_dp, n_ex, share, row_ref, *refs):
    parts, small, refs = refs[:n_ex], refs[n_ex : 2 * n_ex], refs[2 * n_ex :]
    out_refs, all_ref = refs[:n_dp], refs[n_dp]
    line = small[0][...]
    for part in small[1:]:
        line = line + part[...]
    upper = line.astype(BF).astype(F32)
    lower = line - upper
    width = line.shape[1]
    for dp in range(n_dp):
        total = parts[0][dp].astype(F32)
        for part in parts[1:]:
            total = total + part[dp].astype(F32)
        all_ref[dp] = total
        all_ref[dp, share : share + 1, :width] = upper[dp : dp + 1, :]
        all_ref[dp, share + 1 : share + 2, :width] = lower[dp : dp + 1, :]
    for i in range(n_dp):
        out_refs[i][...] = all_ref[row_ref[info.to_dp + i]].astype(BF)


def finish_kernel(info, n_dp, share, row_ref, *refs):
    parts, (exit_ref, small_ref, *piece_refs) = refs[:n_dp], refs[n_dp:]
    chunk = info.chunk
    head = whole_tiles(share + 2)
    total = parts[0][...].astype(F32)
    for part in parts[1:]:
        total = total + part[...].astype(F32)
    exit_ref[...] = total[:share, :]
    small = total[share : share + 1, :] + total[share + 1 : share + 2, :]
    small_ref[...] = small[:, : small_ref.shape[1]]
    pieces = [total[head + i * chunk : head + (i + 1) * chunk, :] for i in range(info.per)]
    for i in range(info.per):
        piece_refs[i][...] = chosen(pieces, row_ref[info.send_slot + i])


def close_kernel(info, row_ref, *refs):
    came, entry_ref = refs[: info.per], refs[info.per]
    chunk = info.chunk
    parts = [ref[...] for ref in came]
    for i in range(info.per):
        entry_ref[i * chunk : (i + 1) * chunk, :] = chosen(parts, row_ref[info.sub_round + i])


def allowed_of(docs_row, docs_col, start, rows, keys):
    query = start + lax.broadcasted_iota(jnp.int32, (rows, keys), 0)
    key = lax.broadcasted_iota(jnp.int32, (rows, keys), 1)
    return (key <= query) & (docs_col[start : start + rows, :] == docs_row[:, :keys])


def bias_rows(lag_ref, head, start, rows, keys):
    length = lag_ref.shape[1]
    flat = jnp.broadcast_to(lag_ref[head : head + 1, :], (rows, length))
    return pltpu.roll(flat, start, 1, stride=1, stride_axis=0)[:, :keys]


def aligned(block, index):
    return pl.ds(pl.multiple_of(index * block, block), block)


def attend_kernel(info, heads, size, count, row_ref, *refs):
    x_refs, refs = refs[:count], refs[count:]
    gain_ref, w_ref, doc_ref, col_ref, lag_ref, x_ref, qkv_ref, ctx_ref, log_ref = refs
    length = x_ref.shape[0]
    rows = length // count
    width = heads * size
    factor = size ** (-0.5)
    for i in range(count):
        x_ref[aligned(rows, row_ref[info.from_seq + i]), :] = x_refs[i][...]
    normed = (x_ref[...].astype(F32) * gain_ref[0:1, :]).astype(BF)
    qkv_ref[...] = dot(normed, w_ref[...], 1, 1).astype(BF)
    for start in range(0, length, BLOCK):
        keys = start + BLOCK
        allowed = allowed_of(doc_ref, col_ref, start, BLOCK, keys)
        for head in range(heads):
            lo = head * size
            q = qkv_ref[start:keys, lo : lo + size]
            k = qkv_ref[:keys, width + lo : width + lo + size]
            v = qkv_ref[:keys, 2 * width + lo : 2 * width + lo + size]
            scores = dot(q, k, 1, 1) * factor + bias_rows(lag_ref, head, start, BLOCK, keys)
            scores = jnp.where(allowed, scores, MASKED)
            peak = jnp.max(scores, axis=1, keepdims=True)
            raised = jnp.exp(scores - peak)
            total = jnp.sum(raised, axis=1, keepdims=True)
            weights = (raised / total).astype(BF)
            log_ref[start:keys, head : head + 1] = peak + jnp.log(total)
            ctx_ref[start:keys, lo : lo + size] = dot(weights, v, 1, 0).astype(BF)


def attend(info, heads, size, info_row, blocks, gain, w, docs_row, docs_col, lag):
    count = len(blocks)
    rows, features = blocks[0].shape
    length = rows * count
    width = heads * size
    return small_call(
        functools.partial(attend_kernel, info, heads, size, count),
        info_row,
        (*blocks, gain, w, docs_row, docs_col, lag),
        [
            ((length, features), BF),
            ((length, 3 * width), BF),
            ((length, width), BF),
            ((length, heads), F32),
        ],
        [],
    )


def leave_kernel(info, n_dp, n_seq, n_ex, row_ref, ctx_ref, *refs):
    exits, refs = refs[:n_seq], refs[n_seq:]
    exit_ref, part_refs, (four_ref, line_ref) = refs[0], refs[1 : 1 + n_seq], refs[1 + n_seq :]
    rows = part_refs[0].shape[0]
    share = exits[0].shape[1]
    for i in range(n_seq):
        four_ref[row_ref[info.from_seq + i]] = exits[i][...].astype(F32)
    for dp in range(n_dp):
        for seq in range(n_seq):
            for ex in range(n_ex):
                start = ((dp * n_seq + seq) * n_ex + ex) * share
                line_ref[start : start + share, :] = four_ref[seq, ex * n_dp + dp]
    exit_ref[...] = line_ref[...].astype(BF)
    for i, part_ref in enumerate(part_refs):
        block = aligned(rows, row_ref[info.to_seq + i])
        part_ref[...] = dot(ctx_ref[block, :], exit_ref[...], 1, 1).astype(BF)


def leave(info, n_dp, n_seq, n_ex, info_row, ctx, exits):
    spots, share, width = exits[0].shape
    features = spots * share * n_seq
    out = small_call(
        functools.partial(leave_kernel, info, n_dp, n_seq, n_ex),
        info_row,
        (ctx, *exits),
        [((features, width), BF)] + [((ctx.shape[0] // n_seq, features), BF)] * n_seq,
        [((n_seq, spots, share, width), F32), ((features, width), F32)],
    )
    return out[0], out[1:]


def leave_back_kernel(info, count, n_dp, share, row_ref, *refs):
    up_refs, refs = refs[:count], refs[count:]
    ctx_ref, up_ref, *grad_refs, all_ref = refs
    rows = up_refs[0].shape[0]
    for i in range(count):
        up_ref[aligned(rows, row_ref[info.from_seq + i]), :] = up_refs[i][...]
    grad = dot(up_ref[...], ctx_ref[...], 0, 0)
    for dp in range(n_dp):
        for i in range(count):
            start = (dp * count + i) * share
            all_ref[i, dp] = grad[start : start + share, :]
    for i in range(count):
        grad_refs[i][...] = all_ref[row_ref[info.to_seq + i]].astype(BF)


def leave_back(info, n_dp, info_row, blocks, ctx):
    count = len(blocks)
    rows, features = blocks[0].shape
    share = features // (n_dp * count)
    width = ctx.shape[1]
    return small_call(
        functools.partial(leave_back_kernel, info, count, n_dp, share),
        info_row,
        (*blocks, ctx),
        [((rows * count, features), BF)] + [((n_dp, share, width), BF)] * count,
        [((count, n_dp, share, width), F32)],
    )


def attend_back_kernel(info, heads, size, count, n_dp, n_ex, share, row_ref, *refs):
    up_ref, exit_ref, qkv_ref, log_ref, doc_ref, col_ref, lag_ref, x_ref, gain_ref, w_ref = refs[:10]
    two_ref, hot_ref, entry_ref, *refs = refs[10:]
    back_refs, small_refs, refs = refs[:count], refs[count : 2 * count], refs[2 * count :]
    bctx_ref, bqkv_ref, bk_ref, bv_ref, lines_ref, diag_ref, four_ref = refs
    length = up_ref.shape[0]
    rows = length // count
    width = heads * size
    factor = size ** (-0.5)
    bctx_ref[...] = dot(up_ref[...], exit_ref[...], 1, 0).astype(BF)
    bk_ref[...] = jnp.zeros_like(bk_ref)
    bv_ref[...] = jnp.zeros_like(bv_ref)
    lines_ref[...] = jnp.zeros_like(lines_ref)
    for start in range(0, length, BLOCK):
        keys = start + BLOCK
        allowed = allowed_of(doc_ref, col_ref, start, BLOCK, keys)
        for head in range(heads):
            lo = head * size
            q = qkv_ref[start:keys, lo : lo + size]
            k = qkv_ref[:keys, width + lo : width + lo + size]
            v = qkv_ref[:keys, 2 * width + lo : 2 * width + lo + size]
            bc = bctx_ref[start:keys, lo : lo + size]
            scores = dot(q, k, 1, 1) * factor + bias_rows(lag_ref, head, start, BLOCK, keys)
            probs = jnp.where(
                allowed, jnp.exp(scores - log_ref[start:keys, head : head + 1]), 0.0
            )
            back_probs = dot(bc, v, 1, 1)
            row_dot = jnp.sum(probs * back_probs, axis=1, keepdims=True)
            back_scores = probs * (back_probs - row_dot)
            scaled = (back_scores * factor).astype(BF)
            bqkv_ref[start:keys, lo : lo + size] = dot(scaled, k, 1, 0).astype(BF)
            bk_ref[:keys, lo : lo + size] += dot(scaled, q, 0, 0)
            bv_ref[:keys, lo : lo + size] += dot(probs.astype(BF), bc, 0, 0)
            lined = jnp.zeros((8, keys), F32)
            for row in range(0, BLOCK, 8):
                lined = lined + pltpu.roll(
                    back_scores[row : row + 8, :], (keys - start - row - 8) % keys, 1
                )
            lines_ref[8 * head : 8 * head + 8, length - keys :] += lined
    for head in range(heads):
        total = jnp.zeros((1, length), F32)
        for row in range(8):
            total = total + pltpu.roll(
                lines_ref[8 * head + row : 8 * head + row + 1, :], 7 - row, 1
            )
        diag_ref[head : head + 1, :] = total
    bqkv_ref[:, width : 2 * width] = bk_ref[...].astype(BF)
    bqkv_ref[:, 2 * width :] = bv_ref[...].astype(BF)
    normed = (x_ref[...].astype(F32) * gain_ref[0:1, :]).astype(BF)
    entry_ref[...] = dot(bqkv_ref[...], normed, 0, 0).astype(BF)
    gain_grad = jnp.zeros((1, x_ref.shape[1]), F32)
    for i in range(count):
        block = aligned(rows, row_ref[info.to_seq + i])
        back = dot(bqkv_ref[block, :], w_ref[...], 1, 0)
        back_refs[i][...] = back.astype(BF)
        gain_grad += jnp.sum(back * x_ref[block, :].astype(F32), axis=0, keepdims=True)
    bias = lax.dot_general(
        diag_ref[...], hot_ref[...], (((1,), (1,)), ((), ())), precision=HIGH,
        preferred_element_type=F32,
    )
    buckets = hot_ref.shape[0]
    four_ref[...] = jnp.zeros_like(four_ref)
    for k in range(heads):
        lane = 2 * share + k * buckets
        four_ref[:, :, lane : lane + buckets] = jnp.broadcast_to(
            bias[k : k + 1, :].reshape(1, 1, buckets), (count, n_ex * n_dp, buckets)
        )
    for seq in range(count):
        for spot in range(n_ex * n_dp):
            ex, dp = divmod(spot, n_dp)
            lane = ((dp * count + seq) * n_ex + ex) * share
            four_ref[seq, spot : spot + 1, :share] = gain_grad[:, lane : lane + share]
            four_ref[seq, spot : spot + 1, share : 2 * share] = two_ref[:, lane : lane + share]
    for i in range(count):
        small_refs[i][...] = four_ref[row_ref[info.to_seq + i]]


def attend_back(
    info, heads, size, count, n_dp, n_ex, share, info_row,
    up, exit_t, qkv, log, docs_row, docs_col, lag, x, gain, w, gain_two_grad, hot,
):
    length, features = up.shape
    width = heads * size
    entry, *rest = small_call(
        functools.partial(attend_back_kernel, info, heads, size, count, n_dp, n_ex, share),
        info_row,
        (up, exit_t, qkv, log, docs_row, docs_col, lag, x, gain, w, gain_two_grad, hot),
        [
            ((3 * width, features), BF),
            *[((length // count, features), BF)] * count,
            *[((n_ex * n_dp, width), F32)] * count,
        ],
        [
            ((length, width), BF),
            ((length, 3 * width), BF),
            ((length, width), F32),
            ((length, width), F32),
            ((8 * heads, length), F32),
            ((heads, length), F32),
            ((count, n_ex * n_dp, width), F32),
        ],
    )
    return entry, rest[:count], rest[count:]


def norm_kernel(row_ref, in_ref, gain_ref, place_ref, *refs):
    parts, (hidden_ref, scale_ref, send_ref) = refs[:-3], refs[-3:]
    hidden = parts[0][...].astype(F32)
    for part in parts[1:]:
        hidden = hidden + part[...].astype(F32)
    hidden = in_ref[...] + hidden
    scale = rms_scale(hidden)
    normed = (hidden * scale * gain_ref[1:2, :]).astype(BF)
    hidden_ref[...] = hidden
    scale_ref[...] = scale
    send_ref[...] = dot(place_ref[...], normed, 1, 0).astype(BF)


def joined(refs):
    return refs[0][...] if len(refs) == 1 else jnp.concatenate([ref[...] for ref in refs], axis=0)


def expert_kernel(tree, *refs):
    rows_ref, up_ref, w_ups, w_downs, back_ref, acts, bbs = jax.tree.unflatten(tree, refs)
    back = None
    for w_up, w_down, act_ref, bb_ref in zip(w_ups, w_downs, acts, bbs):
        w_up, w_down = joined(w_up), joined(w_down)
        before = dot(rows_ref[...], w_up, 1, 0)
        tangent = jnp.tanh(SLOPE * (before + CUBIC * before * before * before))
        act_ref[...] = (0.5 * before * (1.0 + tangent)).astype(BF)
        slope = 0.5 * (1.0 + tangent) + 0.5 * before * (1.0 - tangent * tangent) * SLOPE * (
            1.0 + 3.0 * CUBIC * before * before
        )
        bb_ref[...] = (dot(up_ref[...], w_down, 1, 1) * slope).astype(BF)
        part = dot(bb_ref[...], w_up, 1, 1)
        back = part if back is None else back + part
    back_ref[...] = back.astype(BF)


def tree_call(kernel, inputs, outs):
    tree = jax.tree.structure((*inputs, *outs))
    return pl.pallas_call(
        functools.partial(kernel, tree), out_shape=tuple(jax.tree.leaves(outs))
    )(*jax.tree.leaves(inputs))


def like(shape, kind=BF):
    return jax.ShapeDtypeStruct(shape, kind)


def expert(rows, upstream, w_ups, w_downs):
    count = len(w_ups)
    hidden = w_ups[0][0].shape[1]
    side = [like((rows.shape[0], hidden))] * count
    out = tree_call(expert_kernel, (rows, upstream, w_ups, w_downs), (like(rows.shape), side, side))
    return out[0], out[1 : 1 + count], out[1 + count :]


def result_kernel(tree, *refs):
    groups, w_downs, outs = jax.tree.unflatten(tree, refs)
    w_downs = [joined(w_down) for w_down in w_downs]
    for group, out_ref in zip(groups, outs):
        start = 0
        for acts in group:
            total = dot(acts[0][...], w_downs[0], 1, 0)
            for act, w_down in zip(acts[1:], w_downs[1:]):
                total = total + dot(act[...], w_down, 1, 0)
            out_ref[start : start + total.shape[0], :] = total.astype(BF)
            start += total.shape[0]


def result(groups, w_downs, shape):
    return tree_call(result_kernel, (groups, w_downs), ([like(shape)] * len(groups),))


def grad_kernel(tree, *refs):
    lefts, rights, others, parts = jax.tree.unflatten(tree, refs)
    total = None
    for left, right in zip(lefts, rights):
        part = dot(left[...], right[...], 0, 0)
        total = part if total is None else total + part
    size = total.shape[0] // len(parts)
    for i, part_ref in enumerate(parts):
        part_ref[...] = total[i * size : (i + 1) * size, :].astype(part_ref.dtype)
    for other in others:
        start = 0
        for piece in other:
            stop = start + piece.shape[0]
            parts[0][start:stop, :] += piece[...].astype(F32)
            start = stop


def expert_grad(lefts, rights, kind, pieces=1, others=()):
    shape = (lefts[0].shape[1] // pieces, rights[0].shape[1])
    return tree_call(grad_kernel, (lefts, rights, list(others)), ([like(shape, kind)] * pieces,))


def target(count, me, step):
    return me ^ step if count & (count - 1) == 0 else (me + step) % count


def source(count, me, step):
    return me ^ step if count & (count - 1) == 0 else (me - step) % count


def shift(array, axis, step):
    count = lax.axis_size(axis)
    return lax.ppermute(array, axis, tuple((i, target(count, i, step)) for i in range(count)))


def gathered(array, axis, steps):
    return [array] + [shift(array, axis, step) for step in steps]


def exchanged(array, axis):
    return lax.all_to_all(array, axis, 0, 0, tiled=True)


def traded(blocks, axis, steps):
    return [blocks[0]] + [shift(block, axis, step) for block, step in zip(blocks[1:], steps)]


def summed(blocks, axis, steps):
    came = traded(blocks, axis, steps)
    return functools.reduce(jnp.add, [block.astype(F32) for block in came])


def handed_back(blocks, axis, steps):
    count = lax.axis_size(axis)
    return summed(blocks, axis, tuple(source(count, 0, step) for step in steps))


def after(arrays, *others):
    return lax.optimization_barrier((tuple(arrays), others))[0]


def local(
    block_input,
    documents,
    route_experts,
    route_gate,
    first_gain,
    entry_weight,
    exit_weight,
    position_bias,
    second_gain,
    expert_up,
    expert_down,
    cotangent,
):
    n_dp, n_seq, n_ex = (lax.axis_size(name) for name in ALL)
    group_count = n_dp * n_ex
    rows_here, features = block_input.shape[1:]
    buckets, head_count = position_bias.shape
    size = features // head_count
    heads = head_count // n_seq
    width = heads * size
    top_count = route_experts.shape[2]
    length = rows_here * n_seq
    me = lax.axis_index(ALL)
    here = lax.axis_index("seq")
    inputs = block_input.reshape(rows_here, features)
    upstream = cotangent.reshape(rows_here, features)

    seq_steps = tuple(range(1, n_seq))
    owned = entry_weight.shape[1]
    share = exit_weight.shape[1]
    info = Info(features, owned, n_dp, n_seq, n_ex)
    per, chunk = info.per, info.chunk
    info_row = lax.dynamic_slice(jnp.asarray(info.table), (me, 0), (1, info.table.shape[1]))
    info_row = info_row.reshape(info.table.shape[1])

    pieces = small_call(
        functools.partial(pick_kernel, info),
        info_row, (entry_weight.T,), [((chunk, features), BF)] * per, [],
    )
    came = [lax.ppermute(piece, ALL, pair) for piece, pair in zip(pieces, info.pairs)]
    gains = jnp.pad(jnp.concatenate([first_gain, second_gain]), (0, features - 2 * share))
    group_size = n_dp * n_ex
    capacity = 3 * rows_here // group_size
    slots = group_size * capacity
    route_count = rows_here * top_count
    flat_routes = route_experts.reshape(rows_here, top_count).T.reshape(1, route_count)
    gates = route_gate.reshape(rows_here, top_count)
    named = flat_routes == jnp.arange(group_size, dtype=jnp.int32)[:, None]
    order = jnp.arange(route_count, dtype=jnp.int32)
    earlier = (order[:, None] < order[None, :]).astype(BF)
    rank = jnp.dot(named.astype(BF), earlier, preferred_element_type=F32)
    first = (jnp.arange(group_size, dtype=jnp.int32) * capacity).astype(F32)[:, None]
    slot_of = jnp.sum(jnp.where(named, rank + first, 0.0), axis=0, keepdims=True)
    place = (
        jnp.arange(slots, dtype=jnp.int32)[:, None] == slot_of.astype(jnp.int32)
    ).astype(BF)
    place_each = [place[:, k * rows_here : (k + 1) * rows_here] for k in range(top_count)]
    place_any = functools.reduce(jnp.add, place_each)
    shaped = (group_size, capacity, features)

    gated = jnp.concatenate(
        [(upstream * gates[:, k : k + 1]).astype(BF) for k in range(top_count)], axis=0
    )
    send_upstream = dot(place, gated, 1, 0).astype(BF)
    docs = documents.reshape(length)
    docs_row, docs_col = docs.reshape(1, length), docs.reshape(length, 1)
    lane = jnp.arange(length, dtype=jnp.int32)
    hot = bucket_hot(jnp.where(lane == 0, 0, length - lane), buckets)
    bias_here = lax.dynamic_slice_in_dim(position_bias.T, here * heads, heads)
    lag = jnp.dot(bias_here, hot, precision=HIGH)
    hot_back = bucket_hot(length - 1 - lane, buckets)
    w_own = (expert_up[0], expert_down[0])
    gain_rows = gathered(gains[None], "seq", seq_steps)
    padded = whole_tiles(share + n_seq) + whole_tiles(owned, 8)
    (weights,) = small_call(
        functools.partial(place_kernel, info, n_seq, share),
        info_row, (*came, exit_weight.T, *gain_rows),
        [((padded, features), BF)], [((padded, features), F32)],
    )
    later, *w_later = after((inputs, *w_own), weights)
    w_cut = [half for w in w_later for half in jnp.split(w, 2)]
    scale_one = rms_scale(later)
    xhats = gathered((later * scale_one).astype(BF), "seq", seq_steps)
    weights = gathered(weights, "dp", range(1, n_dp))
    weights = [block for weight in weights for block in gathered(weight, "expert", range(1, n_ex))]
    entry_t, gains, *exits = small_call(
        functools.partial(arrange_kernel, info, n_dp, n_seq, n_ex, share, owned),
        info_row, weights,
        [((3 * width, features), BF), ((2, features), F32)]
        + [((group_count, share, width), BF)] * n_seq,
        [
            ((group_count, padded, features), BF),
            ((3 * width, features), F32),
            ((n_seq, group_count, share, width), F32),
        ],
    )
    gain_one, gain_two = gains[0:1], gains[1:2]
    exits = exits[:1] + [shift(part, "seq", step) for part, step in zip(exits[1:], seq_steps)]

    inner = 2 if n_seq > 1 and n_seq & (n_seq - 1) == 0 else 1
    in_steps = tuple(range(1, inner))
    out_steps = tuple(range(inner, n_seq, inner))
    w_ups, w_downs = [[w_own[0]]], [[w_own[1]]]
    for step in out_steps:
        cut = [shift(half, "seq", step) for half in w_cut]
        w_ups.append(cut[:2])
        w_downs.append(cut[2:])

    came_upstream = exchanged(send_upstream.reshape(shaped), GROUP).reshape(slots, features)

    (lag,) = after((lag,), send_upstream)
    xfull, qkv, ctx, log = attend(
        info, heads, size, info_row, xhats, gains, entry_t, docs_row, docs_col, lag
    )
    exit_t, parts = leave(info, n_dp, n_seq, n_ex, info_row, ctx, exits)

    hidden, scale_two, send_rows = small_call(
        norm_kernel,
        info_row,
        (inputs, gains, place_any, *traded(parts, "seq", seq_steps)),
        [((rows_here, features), F32), ((rows_here, 1), F32), ((slots, features), BF)],
        [],
    )

    came_rows = exchanged(send_rows.reshape(shaped), GROUP).reshape(slots, features)
    rows, ups = [came_rows], [came_upstream]
    for step in in_steps:
        for j in range(2):
            part = slice(j * slots // 2, (j + 1) * slots // 2)
            ups.append(shift(came_upstream[part], "seq", step))
            rows.append(shift(came_rows[part], "seq", step))
    worked = []
    for m in range(1, len(rows)):
        worked.append(expert(rows[m], ups[m], w_ups, w_downs))
    own = []
    for j in range(len(w_ups)):
        own.append(expert(rows[0], ups[0], w_ups[j : j + 1], w_downs[j : j + 1]))
    back_sum = sum(o[0].astype(F32) for o in own)
    for i, step in enumerate(in_steps):
        parts = [shift(worked[2 * i + j][0], "seq", source(n_seq, 0, step)) for j in range(2)]
        back_sum = back_sum + jnp.concatenate(parts).astype(F32)
    back_sum = back_sum.astype(BF)
    returned_back = exchanged(back_sum.reshape(shaped), GROUP).reshape(slots, features)
    own_acts = [o[1][0] for o in own]
    own_bbs = [o[2][0] for o in own]
    groups = [[own_acts]] + [
        [worked[2 * i + j][1] for j in range(2)] for i in range(len(in_steps))
    ]
    results = result(groups, w_downs, came_rows.shape)
    all_acts = [[own_acts[j]] + [w[1][j] for w in worked] for j in range(len(w_ups))]
    all_bbs = [[own_bbs[j]] + [w[2][j] for w in worked] for j in range(len(w_ups))]
    came_ups, came_downs = [], []
    for i, step in enumerate(out_steps):
        step = source(n_seq, 0, step)
        part = expert_grad(rows, all_bbs[i + 1], BF, 2)
        came_ups.append([shift(p, "seq", step) for p in part])
        part = expert_grad(all_acts[i + 1], ups, BF, 2)
        came_downs.append([shift(p, "seq", step) for p in part])

    back_normed_two = dot(place_any, returned_back, 0, 0)
    upper_two = back_normed_two * gain_two
    gain_two_grad = jnp.sum(back_normed_two * hidden * scale_two, axis=0, keepdims=True)
    back_hidden = upstream + scale_two * (
        upper_two
        - hidden * scale_two * scale_two * jnp.mean(upper_two * hidden, axis=1, keepdims=True)
    )
    up_hiddens = gathered(back_hidden.astype(BF), "seq", seq_steps)

    out_sum = handed_back(results, "seq", in_steps).astype(BF)
    returned_out = exchanged(out_sum.reshape(shaped), GROUP).reshape(slots, features)
    block_output = hidden
    for k in range(top_count):
        block_output = block_output + dot(place_each[k], returned_out, 0, 0) * gates[:, k : k + 1]

    up_full, *exit_grads = leave_back(info, n_dp, info_row, up_hiddens, ctx)
    exit_grads = exit_grads[:1] + [
        shift(part, "seq", step)
        for part, step in zip(exit_grads[1:], seq_steps)
    ]
    entry_grad, backs, smalls = attend_back(
        info, heads, size, n_seq, n_dp, n_ex, share, info_row, up_full, exit_t, qkv, log,
        docs_row, docs_col, lag, xfull, gains, entry_t, gain_two_grad, hot_back,
    )

    smalls = traded(smalls, "seq", seq_steps)
    wide = -(-(2 * share + head_count * buckets) // 128) * 128
    assert wide <= features and 2 * share + heads * buckets <= width
    padded = whole_tiles(share + 2) + whole_tiles(owned, 8)
    halves = small_call(
        functools.partial(pack_kernel, info, n_dp, n_seq, n_ex, share, owned),
        info_row,
        (*exit_grads, entry_grad),
        [((n_dp, padded, features), BF)] * n_ex,
        [
            ((n_seq, n_dp, n_ex * share, width), F32),
            ((n_ex, n_dp, padded, features), F32),
        ],
    )
    halves = traded(halves, "expert", range(1, n_ex))
    smalls = small_call(
        functools.partial(small_kernel, info, n_dp, n_seq, n_ex, share, heads, buckets),
        info_row,
        smalls,
        [((n_dp, wide), F32)] * n_ex,
        [((n_seq, n_ex * n_dp, width), F32), ((n_ex, n_dp, wide), F32)],
    )
    smalls = traded(smalls, "expert", range(1, n_ex))
    quarters = small_call(
        functools.partial(fold_kernel, info, n_dp, n_ex, share),
        info_row,
        (*halves, *smalls),
        [((padded, features), BF)] * n_dp,
        [((n_dp, padded, features), F32)],
    )
    folded = quarters
    quarters = traded(quarters, "dp", range(1, n_dp))
    exit_share, small, *pieces = small_call(
        functools.partial(finish_kernel, info, n_dp, share),
        info_row,
        quarters,
        [((share, features), F32), ((1, wide), F32)] + [((chunk, features), F32)] * per,
        [],
    )
    came = [
        lax.ppermute(piece, ALL, tuple((b, a) for a, b in pair))
        for piece, pair in zip(pieces, info.pairs)
    ]
    (entry_share,) = small_call(
        functools.partial(close_kernel, info), info_row, came, [((owned, features), F32)], []
    )
    entry_share, exit_share = entry_share.T, exit_share.T
    small = small[0]
    gain_one_share, gain_two_share = small[:share], small[share : 2 * share]
    bias_total = small[2 * share : 2 * share + head_count * buckets].reshape(head_count, buckets).T

    back_normed_one = summed(backs, "seq", seq_steps)
    upper_one = back_normed_one * gain_one
    back_input = back_hidden + scale_one * (
        upper_one
        - inputs * scale_one * scale_one * jnp.mean(upper_one * inputs, axis=1, keepdims=True)
    )

    own_bb, own_act = after((all_bbs[0][0], all_acts[0][0]), folded)
    (up_grad,) = expert_grad(rows, [own_bb] + all_bbs[0][1:], F32, 1, came_ups)
    (down_grad,) = expert_grad([own_act] + all_acts[0][1:], ups, F32, 1, came_downs)
    return (
        block_output.reshape(block_input.shape),
        back_input.reshape(block_input.shape),
        gain_one_share,
        entry_share,
        exit_share,
        bias_total,
        gain_two_share,
        up_grad[None],
        down_grad[None],
    )


def solution(mesh):
    tokens = P(("dp", "expert"), "seq", None)
    columns = P(None, ALL)
    placed = (
        tokens,
        P(("dp", "expert"), None),
        tokens,
        tokens,
        P(ALL),
        columns,
        columns,
        P(),
        P(ALL),
        P(("dp", "expert"), None, "seq"),
        P(("dp", "expert"), "seq", None),
        tokens,
    )

    return jax.shard_map(
        local,
        mesh=mesh,
        in_specs=placed,
        out_specs=(
            tokens,
            tokens,
            P(ALL),
            columns,
            columns,
            P(),
            P(ALL),
            P(("dp", "expert"), None, "seq"),
            P(("dp", "expert"), "seq", None),
        ),
        check_vma=False,
    )
```

```python
import functools
import math

import jax
import jax.numpy as jnp
import numpy as np
from jax import lax
from jax.experimental import pallas as pl
from jax.experimental.pallas import tpu as pltpu
from jax.sharding import PartitionSpec as P

EPSILON = 1e-06
SLOPE = 0.7978845608028654
CUBIC = 0.044715
LIMITS = (19, 21, 24, 27, 31, 35, 40, 46, 52, 59, 67, 77, 87, 99, 113)
MASKED = -1e30
HIGH = lax.Precision.HIGHEST
ALL = ("dp", "seq", "expert")
GROUP = ("dp", "expert")
BLOCK = 128
BF = jnp.bfloat16
F32 = jnp.float32


def dot(left, right, left_dim, right_dim):
    return lax.dot_general(
        left, right, (((left_dim,), (right_dim,)), ((), ())), preferred_element_type=F32
    )


def rms_scale(values):
    return lax.rsqrt(jnp.mean(values * values, axis=-1, keepdims=True) + EPSILON)


def bucket_hot(lag, count):
    bucket = jnp.minimum(lag, 16)
    for threshold in LIMITS:
        bucket = bucket + (lag >= threshold).astype(jnp.int32)
    return (jnp.arange(count, dtype=jnp.int32)[:, None] == bucket[None, :]).astype(F32)


@functools.lru_cache(maxsize=None)
def weight_routes(features, columns, n_dp, n_seq, n_ex):
    width = features // n_seq
    chunk = math.gcd(columns, width)
    per = columns // chunk
    devices = n_dp * n_seq * n_ex
    edges = []
    for group in range(n_seq):
        index = 0
        for part in range(3):
            for i in range(width // chunk):
                piece = (part * features + group * width) // chunk + i
                ex, rest = divmod(index, n_dp * per)
                dp, slot = divmod(rest, per)
                target = (dp * n_seq + group) * n_ex + ex
                edges.append((piece // per, piece % per, target, slot))
                index += 1
    rounds = []
    left = list(edges)
    for _ in range(per):
        out_edges = [[] for _ in range(devices)]
        for edge in left:
            out_edges[edge[0]].append(edge)
        matched = {}

        def place(source, seen):
            for edge in out_edges[source]:
                if edge[2] in seen:
                    continue
                seen.add(edge[2])
                if edge[2] not in matched or place(matched[edge[2]][0], seen):
                    matched[edge[2]] = edge
                    return True
            return False

        for source in range(devices):
            assert place(source, set())
        rounds.append(sorted(matched.values()))
        for edge in matched.values():
            left.remove(edge)
    pairs = tuple(tuple((e[0], e[2]) for e in r) for r in rounds)
    send = np.zeros((devices, per), np.int32)
    receive = np.zeros((devices, per), np.int32)
    for m, r in enumerate(rounds):
        for source, sub, target, slot in r:
            send[source, m] = sub
            receive[target, slot] = m
    return chunk, per, pairs, send, receive


def inverse_rows(table):
    return np.argsort(table, axis=1).astype(np.int32)


def positions_of(count, sign):
    me, step = np.arange(count)[:, None], np.arange(count)[None, :]
    return me ^ step if count & (count - 1) == 0 else (me + sign * step) % count


class Info:
    def __init__(self, features, columns, n_dp, n_seq, n_ex):
        self.chunk, self.per, self.pairs, send, receive = weight_routes(
            features, columns, n_dp, n_seq, n_ex
        )
        device = np.arange(n_dp * n_seq * n_ex)
        dp, seq, ex = device // (n_seq * n_ex), device // n_ex % n_seq, device % n_ex
        self.width = 0
        self.columns = []
        self.send_sub = self.add(send)
        self.slot_round = self.add(receive)
        self.sub_round = self.add(inverse_rows(send))
        self.send_slot = self.add(inverse_rows(receive))
        self.from_seq = self.add(positions_of(n_seq, -1)[seq])
        self.to_seq = self.add(positions_of(n_seq, 1)[seq])
        self.from_dp = self.add(positions_of(n_dp, -1)[dp])
        self.to_dp = self.add(positions_of(n_dp, 1)[dp])
        self.from_ex = self.add(positions_of(n_ex, -1)[ex])
        self.to_ex = self.add(positions_of(n_ex, 1)[ex])
        self.table = np.concatenate(self.columns, axis=1).astype(np.int32)

    def add(self, part):
        self.columns.append(part)
        self.width += part.shape[1]
        return self.width - part.shape[1]


def chosen(values, index):
    out = values[0]
    for i in range(1, len(values)):
        out = jnp.where(index == i, values[i], out)
    return out


def specs(arrays):
    return [pl.BlockSpec(memory_space=pltpu.SMEM)] + [
        pl.BlockSpec(memory_space=pltpu.VMEM)
    ] * arrays


def small_call(kernel, info_row, arrays, outs, scratch):
    return pl.pallas_call(
        kernel,
        in_specs=specs(len(arrays)),
        out_shape=tuple(jax.ShapeDtypeStruct(shape, kind) for shape, kind in outs),
        scratch_shapes=[pltpu.VMEM(shape, kind) for shape, kind in scratch],
    )(info_row, *arrays)


def whole_tiles(rows, tile=16):
    return -(-rows // tile) * tile


def pick_kernel(info, n_seq, share, row_ref, entry_ref, exit_ref, gain_ref, *refs):
    piece_refs, tiny_refs, four_ref = refs[: info.per], refs[info.per : -1], refs[-1]
    entry = entry_ref[...].astype(F32)
    chunk = info.chunk
    parts = [entry[i * chunk : (i + 1) * chunk, :] for i in range(info.per)]
    for i, piece_ref in enumerate(piece_refs):
        piece_ref[...] = chosen(parts, row_ref[info.send_sub + i]).astype(BF)
    width = four_ref.shape[2]
    leaving = exit_ref[...].astype(F32)
    four_ref[...] = jnp.zeros_like(four_ref)
    for seq in range(n_seq):
        four_ref[seq, :share, :] = leaving[:, seq * width : (seq + 1) * width]
        four_ref[seq, share : share + 1, :] = gain_ref[...].astype(F32)
    for i in range(n_seq):
        tiny_refs[i][...] = four_ref[row_ref[info.to_seq + i]].astype(BF)


def place_kernel(info, n_seq, share, row_ref, *refs):
    per, chunk = info.per, info.chunk
    came, tiny = refs[:per], refs[per : per + n_seq]
    out_ref, line_ref, four_ref = refs[per + n_seq :]
    head = whole_tiles(share + n_seq)
    width = four_ref.shape[2]
    line_ref[...] = jnp.zeros_like(line_ref)
    for i in range(n_seq):
        four_ref[row_ref[info.from_seq + i]] = tiny[i][...].astype(F32)
    for seq in range(n_seq):
        line_ref[:share, seq * width : (seq + 1) * width] = four_ref[seq, :share, :]
        line_ref[share + seq : share + seq + 1, :width] = four_ref[seq, share : share + 1, :]
    parts = [ref[...].astype(F32) for ref in came]
    for i in range(per):
        line_ref[head + i * chunk : head + (i + 1) * chunk, :] = chosen(
            parts, row_ref[info.slot_round + i]
        )
    out_ref[...] = line_ref[...].astype(BF)


def arrange_kernel(info, n_dp, n_seq, n_ex, share, owned, row_ref, *refs):
    blocks, refs = refs[: n_dp * n_ex], refs[n_dp * n_ex :]
    entry_ref, gain_ref, exit_ref, all_ref, line_ref, exit_line_ref = refs
    width = exit_ref.shape[1]
    head = whole_tiles(share + n_seq)
    for i in range(n_dp):
        for j in range(n_ex):
            spot = row_ref[info.from_ex + j] * n_dp + row_ref[info.from_dp + i]
            all_ref[spot] = blocks[i * n_ex + j][...]
    for spot in range(n_ex * n_dp):
        ex, dp = divmod(spot, n_dp)
        value = all_ref[spot].astype(F32)
        line_ref[spot * owned : (spot + 1) * owned, :] = value[head : head + owned, :]
        for seq in range(n_seq):
            lane = ((dp * n_seq + seq) * n_ex + ex) * share
            exit_line_ref[lane : lane + share, :] = value[:share, seq * width : (seq + 1) * width]
            for k in range(2):
                gain_ref[k : k + 1, lane : lane + share] = value[
                    share + seq : share + seq + 1, k * share : (k + 1) * share
                ]
    entry_ref[...] = line_ref[...].astype(BF)
    exit_ref[...] = exit_line_ref[...].astype(BF)


def pack_kernel(info, n_dp, n_seq, n_ex, share, owned, row_ref, *refs):
    exits, refs = refs[:n_seq], refs[n_seq:]
    entry_ref, out_refs, (four_ref, all_ref) = refs[0], refs[1 : 1 + n_ex], refs[1 + n_ex :]
    width = exits[0].shape[2]
    head = whole_tiles(share + 2)
    for i in range(n_seq):
        four_ref[row_ref[info.from_seq + i]] = exits[i][...].astype(F32)
    all_ref[...] = jnp.zeros_like(all_ref)
    entry = entry_ref[...].astype(F32)
    for spot in range(n_ex * n_dp):
        ex, dp = divmod(spot, n_dp)
        for seq in range(n_seq):
            to = seq * width
            all_ref[ex, dp, :share, to : to + width] = four_ref[
                seq, dp, ex * share : (ex + 1) * share, :
            ]
        all_ref[ex, dp, head : head + owned, :] = entry[spot * owned : (spot + 1) * owned, :]
    for i in range(n_ex):
        out_refs[i][...] = all_ref[row_ref[info.to_ex + i]].astype(BF)


def small_kernel(info, n_dp, n_seq, n_ex, share, heads, buckets, row_ref, *refs):
    small, out_refs, (four_ref, all_ref) = refs[:n_seq], refs[n_seq:-2], refs[-2:]
    for i in range(n_seq):
        four_ref[row_ref[info.from_seq + i]] = small[i][...]
    total = four_ref[0]
    for seq in range(1, n_seq):
        total = total + four_ref[seq]
    all_ref[...] = jnp.zeros_like(all_ref)
    part = heads * buckets
    for ex in range(n_ex):
        lines = slice(ex * n_dp, (ex + 1) * n_dp)
        all_ref[ex, :, : 2 * share] = total[lines, : 2 * share]
        for seq in range(n_seq):
            lane = 2 * share + seq * part
            all_ref[ex, :, lane : lane + part] = four_ref[seq, lines, 2 * share : 2 * share + part]
    for i in range(n_ex):
        out_refs[i][...] = all_ref[row_ref[info.to_ex + i]]


def fold_kernel(info, n_dp, n_ex, share, row_ref, *refs):
    parts, small, refs = refs[:n_ex], refs[n_ex : 2 * n_ex], refs[2 * n_ex :]
    out_refs, all_ref = refs[:n_dp], refs[n_dp]
    line = small[0][...]
    for part in small[1:]:
        line = line + part[...]
    upper = line.astype(BF).astype(F32)
    lower = line - upper
    width = line.shape[1]
    for dp in range(n_dp):
        total = parts[0][dp].astype(F32)
        for part in parts[1:]:
            total = total + part[dp].astype(F32)
        all_ref[dp] = total
        all_ref[dp, share : share + 1, :width] = upper[dp : dp + 1, :]
        all_ref[dp, share + 1 : share + 2, :width] = lower[dp : dp + 1, :]
    for i in range(n_dp):
        out_refs[i][...] = all_ref[row_ref[info.to_dp + i]].astype(BF)


def finish_kernel(info, n_dp, share, row_ref, *refs):
    parts, (exit_ref, small_ref, *piece_refs) = refs[:n_dp], refs[n_dp:]
    chunk = info.chunk
    head = whole_tiles(share + 2)
    total = parts[0][...].astype(F32)
    for part in parts[1:]:
        total = total + part[...].astype(F32)
    exit_ref[...] = total[:share, :]
    small = total[share : share + 1, :] + total[share + 1 : share + 2, :]
    small_ref[...] = small[:, : small_ref.shape[1]]
    pieces = [total[head + i * chunk : head + (i + 1) * chunk, :] for i in range(info.per)]
    for i in range(info.per):
        piece_refs[i][...] = chosen(pieces, row_ref[info.send_slot + i])


def close_kernel(info, row_ref, *refs):
    came, entry_ref = refs[: info.per], refs[info.per]
    chunk = info.chunk
    parts = [ref[...] for ref in came]
    for i in range(info.per):
        entry_ref[i * chunk : (i + 1) * chunk, :] = chosen(parts, row_ref[info.sub_round + i])


def allowed_of(docs_row, docs_col, start, rows, keys):
    query = start + lax.broadcasted_iota(jnp.int32, (rows, keys), 0)
    key = lax.broadcasted_iota(jnp.int32, (rows, keys), 1)
    return (key <= query) & (docs_col[start : start + rows, :] == docs_row[:, :keys])


def bias_rows(lag_ref, head, start, rows, keys):
    length = lag_ref.shape[1]
    line = lag_ref[head : head + 1, length - keys :]
    lane = lax.broadcasted_iota(jnp.int32, (1, keys), 1)
    line = jnp.where(lane == 0, lag_ref[head : head + 1, :1], line)
    flat = jnp.broadcast_to(line, (rows, keys))
    return pltpu.roll(flat, start, 1, stride=1, stride_axis=0)


def aligned(block, index):
    return pl.ds(pl.multiple_of(index * block, block), block)


def attend_kernel(info, heads, size, count, row_ref, *refs):
    x_refs, refs = refs[:count], refs[count:]
    gain_ref, w_ref, doc_ref, col_ref, lag_ref, x_ref, qkv_ref, ctx_ref, log_ref = refs
    length = x_ref.shape[0]
    rows = length // count
    width = heads * size
    factor = size ** (-0.5)
    for i in range(count):
        x_ref[aligned(rows, row_ref[info.from_seq + i]), :] = x_refs[i][...]
    normed = (x_ref[...].astype(F32) * gain_ref[0:1, :]).astype(BF)
    qkv_ref[...] = dot(normed, w_ref[...], 1, 1).astype(BF)
    for start in range(0, length, BLOCK):
        keys = start + BLOCK
        allowed = allowed_of(doc_ref, col_ref, start, BLOCK, keys)
        for head in range(heads):
            lo = head * size
            q = qkv_ref[start:keys, lo : lo + size]
            k = qkv_ref[:keys, width + lo : width + lo + size]
            v = qkv_ref[:keys, 2 * width + lo : 2 * width + lo + size]
            scores = dot(q, k, 1, 1) * factor + bias_rows(lag_ref, head, start, BLOCK, keys)
            scores = jnp.where(allowed, scores, MASKED)
            peak = jnp.max(scores, axis=1, keepdims=True)
            raised = jnp.exp(scores - peak)
            total = jnp.sum(raised, axis=1, keepdims=True)
            weights = (raised / total).astype(BF)
            log_ref[start:keys, head : head + 1] = peak + jnp.log(total)
            ctx_ref[start:keys, lo : lo + size] = dot(weights, v, 1, 0).astype(BF)


def attend(info, heads, size, info_row, blocks, gain, w, docs_row, docs_col, lag):
    count = len(blocks)
    rows, features = blocks[0].shape
    length = rows * count
    width = heads * size
    return small_call(
        functools.partial(attend_kernel, info, heads, size, count),
        info_row,
        (*blocks, gain, w, docs_row, docs_col, lag),
        [
            ((length, features), BF),
            ((length, 3 * width), BF),
            ((length, width), BF),
            ((length, heads), F32),
        ],
        [],
    )


def leave_kernel(info, row_ref, ctx_ref, exit_ref, *part_refs):
    rows = part_refs[0].shape[0]
    for i, part_ref in enumerate(part_refs):
        block = aligned(rows, row_ref[info.to_seq + i])
        part_ref[...] = dot(ctx_ref[block, :], exit_ref[...], 1, 1).astype(BF)


def leave(info, n_seq, info_row, ctx, exit_t):
    return small_call(
        functools.partial(leave_kernel, info),
        info_row,
        (ctx, exit_t),
        [((ctx.shape[0] // n_seq, exit_t.shape[0]), BF)] * n_seq,
        [],
    )


def leave_back_kernel(info, count, n_dp, share, row_ref, *refs):
    up_refs, refs = refs[:count], refs[count:]
    ctx_ref, up_ref, *grad_refs, all_ref = refs
    rows = up_refs[0].shape[0]
    for i in range(count):
        up_ref[aligned(rows, row_ref[info.from_seq + i]), :] = up_refs[i][...]
    grad = dot(up_ref[...], ctx_ref[...], 0, 0)
    for dp in range(n_dp):
        for i in range(count):
            start = (dp * count + i) * share
            all_ref[i, dp] = grad[start : start + share, :]
    for i in range(count):
        grad_refs[i][...] = all_ref[row_ref[info.to_seq + i]].astype(BF)


def leave_back(info, n_dp, info_row, blocks, ctx):
    count = len(blocks)
    rows, features = blocks[0].shape
    share = features // (n_dp * count)
    width = ctx.shape[1]
    return small_call(
        functools.partial(leave_back_kernel, info, count, n_dp, share),
        info_row,
        (*blocks, ctx),
        [((rows * count, features), BF)] + [((n_dp, share, width), BF)] * count,
        [((count, n_dp, share, width), F32)],
    )


def attend_back_kernel(info, heads, size, count, n_dp, n_ex, share, row_ref, *refs):
    up_ref, exit_ref, qkv_ref, log_ref, doc_ref, col_ref, lag_ref, x_ref, gain_ref, w_ref = refs[:10]
    two_ref, hot_ref, entry_ref, *refs = refs[10:]
    back_refs, small_refs, refs = refs[:count], refs[count : 2 * count], refs[2 * count :]
    bctx_ref, bqkv_ref, bk_ref, bv_ref, lines_ref, diag_ref, four_ref = refs
    length = up_ref.shape[0]
    rows = length // count
    width = heads * size
    factor = size ** (-0.5)
    bctx_ref[...] = dot(up_ref[...], exit_ref[...], 1, 0).astype(BF)
    bk_ref[...] = jnp.zeros_like(bk_ref)
    bv_ref[...] = jnp.zeros_like(bv_ref)
    lines_ref[...] = jnp.zeros_like(lines_ref)
    for start in range(0, length, BLOCK):
        keys = start + BLOCK
        allowed = allowed_of(doc_ref, col_ref, start, BLOCK, keys)
        for head in range(heads):
            lo = head * size
            q = qkv_ref[start:keys, lo : lo + size]
            k = qkv_ref[:keys, width + lo : width + lo + size]
            v = qkv_ref[:keys, 2 * width + lo : 2 * width + lo + size]
            bc = bctx_ref[start:keys, lo : lo + size]
            scores = dot(q, k, 1, 1) * factor + bias_rows(lag_ref, head, start, BLOCK, keys)
            probs = jnp.where(
                allowed, jnp.exp(scores - log_ref[start:keys, head : head + 1]), 0.0
            )
            back_probs = dot(bc, v, 1, 1)
            row_dot = jnp.sum(probs * back_probs, axis=1, keepdims=True)
            back_scores = probs * (back_probs - row_dot)
            scaled = (back_scores * factor).astype(BF)
            bqkv_ref[start:keys, lo : lo + size] = dot(scaled, k, 1, 0).astype(BF)
            bk_ref[:keys, lo : lo + size] += dot(scaled, q, 0, 0)
            bv_ref[:keys, lo : lo + size] += dot(probs.astype(BF), bc, 0, 0)
            lined = jnp.zeros((8, keys), F32)
            for row in range(0, BLOCK, 8):
                lined = lined + pltpu.roll(
                    back_scores[row : row + 8, :], (keys - start - row - 8) % keys, 1
                )
            lines_ref[8 * head : 8 * head + 8, length - keys :] += lined
    for head in range(heads):
        total = jnp.zeros((1, length), F32)
        for row in range(8):
            total = total + pltpu.roll(
                lines_ref[8 * head + row : 8 * head + row + 1, :], 7 - row, 1
            )
        diag_ref[head : head + 1, :] = total
    bqkv_ref[:, width : 2 * width] = bk_ref[...].astype(BF)
    bqkv_ref[:, 2 * width :] = bv_ref[...].astype(BF)
    normed = (x_ref[...].astype(F32) * gain_ref[0:1, :]).astype(BF)
    entry_ref[...] = dot(bqkv_ref[...], normed, 0, 0).astype(BF)
    gain_grad = jnp.zeros((1, x_ref.shape[1]), F32)
    for i in range(count):
        block = aligned(rows, row_ref[info.to_seq + i])
        back = dot(bqkv_ref[block, :], w_ref[...], 1, 0)
        back_refs[i][...] = back.astype(BF)
        gain_grad += jnp.sum(back * x_ref[block, :].astype(F32), axis=0, keepdims=True)
    bias = lax.dot_general(
        diag_ref[...], hot_ref[...], (((1,), (1,)), ((), ())), precision=HIGH,
        preferred_element_type=F32,
    )
    buckets = hot_ref.shape[0]
    four_ref[...] = jnp.zeros_like(four_ref)
    for k in range(heads):
        lane = 2 * share + k * buckets
        four_ref[:, :, lane : lane + buckets] = jnp.broadcast_to(
            bias[k : k + 1, :].reshape(1, 1, buckets), (count, n_ex * n_dp, buckets)
        )
    for seq in range(count):
        for spot in range(n_ex * n_dp):
            ex, dp = divmod(spot, n_dp)
            lane = ((dp * count + seq) * n_ex + ex) * share
            four_ref[seq, spot : spot + 1, :share] = gain_grad[:, lane : lane + share]
            four_ref[seq, spot : spot + 1, share : 2 * share] = two_ref[:, lane : lane + share]
    for i in range(count):
        small_refs[i][...] = four_ref[row_ref[info.to_seq + i]]


def attend_back(
    info, heads, size, count, n_dp, n_ex, share, info_row,
    up, exit_t, qkv, log, docs_row, docs_col, lag, x, gain, w, gain_two_grad, hot,
):
    length, features = up.shape
    width = heads * size
    entry, *rest = small_call(
        functools.partial(attend_back_kernel, info, heads, size, count, n_dp, n_ex, share),
        info_row,
        (up, exit_t, qkv, log, docs_row, docs_col, lag, x, gain, w, gain_two_grad, hot),
        [
            ((3 * width, features), BF),
            *[((length // count, features), BF)] * count,
            *[((n_ex * n_dp, width), F32)] * count,
        ],
        [
            ((length, width), BF),
            ((length, 3 * width), BF),
            ((length, width), F32),
            ((length, width), F32),
            ((8 * heads, length), F32),
            ((heads, length), F32),
            ((count, n_ex * n_dp, width), F32),
        ],
    )
    return entry, rest[:count], rest[count:]


def norm_kernel(row_ref, in_ref, gain_ref, place_ref, *refs):
    parts, (hidden_ref, scale_ref, send_ref) = refs[:-3], refs[-3:]
    hidden = parts[0][...].astype(F32)
    for part in parts[1:]:
        hidden = hidden + part[...].astype(F32)
    hidden = in_ref[...] + hidden
    scale = rms_scale(hidden)
    normed = (hidden * scale * gain_ref[1:2, :]).astype(BF)
    hidden_ref[...] = hidden
    scale_ref[...] = scale
    send_ref[...] = dot(place_ref[...], normed, 1, 0).astype(BF)


def joined(refs):
    return refs[0][...] if len(refs) == 1 else jnp.concatenate([ref[...] for ref in refs], axis=0)


def expert_kernel(tree, *refs):
    rows_ref, up_ref, w_ups, w_downs, back_ref, acts, bbs = jax.tree.unflatten(tree, refs)
    back = None
    for w_up, w_down, act_ref, bb_ref in zip(w_ups, w_downs, acts, bbs):
        w_up, w_down = joined(w_up), joined(w_down)
        before = dot(rows_ref[...], w_up, 1, 0)
        tangent = jnp.tanh(SLOPE * (before + CUBIC * before * before * before))
        act_ref[...] = (0.5 * before * (1.0 + tangent)).astype(BF)
        slope = 0.5 * (1.0 + tangent) + 0.5 * before * (1.0 - tangent * tangent) * SLOPE * (
            1.0 + 3.0 * CUBIC * before * before
        )
        bb_ref[...] = (dot(up_ref[...], w_down, 1, 1) * slope).astype(BF)
        part = dot(bb_ref[...], w_up, 1, 1)
        back = part if back is None else back + part
    back_ref[...] = back.astype(BF)


def tree_call(kernel, inputs, outs):
    tree = jax.tree.structure((*inputs, *outs))
    return pl.pallas_call(
        functools.partial(kernel, tree), out_shape=tuple(jax.tree.leaves(outs))
    )(*jax.tree.leaves(inputs))


def like(shape, kind=BF):
    return jax.ShapeDtypeStruct(shape, kind)


def expert(rows, upstream, w_ups, w_downs):
    count = len(w_ups)
    hidden = w_ups[0][0].shape[1]
    side = [like((rows.shape[0], hidden))] * count
    out = tree_call(expert_kernel, (rows, upstream, w_ups, w_downs), (like(rows.shape), side, side))
    return out[0], out[1 : 1 + count], out[1 + count :]


def result_kernel(tree, *refs):
    groups, w_downs, outs = jax.tree.unflatten(tree, refs)
    w_downs = [joined(w_down) for w_down in w_downs]
    for group, out_ref in zip(groups, outs):
        start = 0
        for acts in group:
            total = dot(acts[0][...], w_downs[0], 1, 0)
            for act, w_down in zip(acts[1:], w_downs[1:]):
                total = total + dot(act[...], w_down, 1, 0)
            out_ref[start : start + total.shape[0], :] = total.astype(BF)
            start += total.shape[0]


def result(groups, w_downs, shape):
    return tree_call(result_kernel, (groups, w_downs), ([like(shape)] * len(groups),))


def grad_kernel(tree, *refs):
    lefts, rights, others, parts = jax.tree.unflatten(tree, refs)
    total = None
    for left, right in zip(lefts, rights):
        part = dot(left[...], right[...], 0, 0)
        total = part if total is None else total + part
    size = total.shape[0] // len(parts)
    for i, part_ref in enumerate(parts):
        part_ref[...] = total[i * size : (i + 1) * size, :].astype(part_ref.dtype)
    for other in others:
        start = 0
        for piece in other:
            stop = start + piece.shape[0]
            parts[0][start:stop, :] += piece[...].astype(F32)
            start = stop


def expert_grad(lefts, rights, kind, pieces=1, others=()):
    shape = (lefts[0].shape[1] // pieces, rights[0].shape[1])
    return tree_call(grad_kernel, (lefts, rights, list(others)), ([like(shape, kind)] * pieces,))


def target(count, me, step):
    return me ^ step if count & (count - 1) == 0 else (me + step) % count


def source(count, me, step):
    return me ^ step if count & (count - 1) == 0 else (me - step) % count


def shift(array, axis, step):
    count = lax.axis_size(axis)
    return lax.ppermute(array, axis, tuple((i, target(count, i, step)) for i in range(count)))


def gathered(array, axis, steps):
    return [array] + [shift(array, axis, step) for step in steps]


def exchanged(array, axis):
    return lax.all_to_all(array, axis, 0, 0, tiled=True)


def traded(blocks, axis, steps):
    return [blocks[0]] + [shift(block, axis, step) for block, step in zip(blocks[1:], steps)]


def summed(blocks, axis, steps):
    came = traded(blocks, axis, steps)
    return functools.reduce(jnp.add, [block.astype(F32) for block in came])


def handed_back(blocks, axis, steps):
    count = lax.axis_size(axis)
    return summed(blocks, axis, tuple(source(count, 0, step) for step in steps))


def after(arrays, *others):
    return lax.optimization_barrier((tuple(arrays), others))[0]


def local(
    block_input,
    documents,
    route_experts,
    route_gate,
    first_gain,
    entry_weight,
    exit_weight,
    position_bias,
    second_gain,
    expert_up,
    expert_down,
    cotangent,
):
    n_dp, n_seq, n_ex = (lax.axis_size(name) for name in ALL)
    group_count = n_dp * n_ex
    rows_here, features = block_input.shape[1:]
    buckets, head_count = position_bias.shape
    size = features // head_count
    heads = head_count // n_seq
    width = heads * size
    top_count = route_experts.shape[2]
    length = rows_here * n_seq
    me = lax.axis_index(ALL)
    here = lax.axis_index("seq")
    inputs = block_input.reshape(rows_here, features)
    upstream = cotangent.reshape(rows_here, features)

    seq_steps = tuple(range(1, n_seq))
    owned = entry_weight.shape[1]
    share = exit_weight.shape[1]
    info = Info(features, owned, n_dp, n_seq, n_ex)
    per, chunk = info.per, info.chunk
    info_row = lax.dynamic_slice(jnp.asarray(info.table), (me, 0), (1, info.table.shape[1]))
    info_row = info_row.reshape(info.table.shape[1])

    gains = jnp.concatenate([first_gain, second_gain])
    gains = jnp.pad(gains, (0, width - 2 * share))[None]
    lines = whole_tiles(share + 1)
    out = small_call(
        functools.partial(pick_kernel, info, n_seq, share),
        info_row, (entry_weight.T, exit_weight.T, gains),
        [((chunk, features), BF)] * per + [((lines, width), BF)] * n_seq,
        [((n_seq, lines, width), F32)],
    )
    pieces, tiny = out[:per], out[per:]
    came = [lax.ppermute(piece, ALL, pair) for piece, pair in zip(pieces, info.pairs)]
    group_size = n_dp * n_ex
    capacity = 3 * rows_here // group_size
    slots = group_size * capacity
    route_count = rows_here * top_count
    flat_routes = route_experts.reshape(rows_here, top_count).T.reshape(1, route_count)
    gates = route_gate.reshape(rows_here, top_count)
    named = flat_routes == jnp.arange(group_size, dtype=jnp.int32)[:, None]
    order = jnp.arange(route_count, dtype=jnp.int32)
    earlier = (order[:, None] < order[None, :]).astype(BF)
    rank = jnp.dot(named.astype(BF), earlier, preferred_element_type=F32)
    first = (jnp.arange(group_size, dtype=jnp.int32) * capacity).astype(F32)[:, None]
    slot_of = jnp.sum(jnp.where(named, rank + first, 0.0), axis=0, keepdims=True)
    place = (
        jnp.arange(slots, dtype=jnp.int32)[:, None] == slot_of.astype(jnp.int32)
    ).astype(BF)
    place_each = [place[:, k * rows_here : (k + 1) * rows_here] for k in range(top_count)]
    place_any = functools.reduce(jnp.add, place_each)
    shaped = (group_size, capacity, features)

    gated = jnp.concatenate(
        [(upstream * gates[:, k : k + 1]).astype(BF) for k in range(top_count)], axis=0
    )
    send_upstream = dot(place, gated, 1, 0).astype(BF)
    docs = documents.reshape(length)
    docs_row, docs_col = docs.reshape(1, length), docs.reshape(length, 1)
    lane = jnp.arange(length, dtype=jnp.int32)
    hot = bucket_hot(jnp.where(lane == 0, 0, length - lane), buckets)
    bias_here = lax.dynamic_slice_in_dim(position_bias.T, here * heads, heads)
    lag = jnp.dot(bias_here, hot, precision=HIGH)
    hot_back = bucket_hot(length - 1 - lane, buckets)
    w_own = (expert_up[0], expert_down[0])
    tiny = traded(tiny, "seq", seq_steps)
    padded = whole_tiles(share + n_seq) + whole_tiles(owned, 8)
    (weights,) = small_call(
        functools.partial(place_kernel, info, n_seq, share),
        info_row, (*came, *tiny),
        [((padded, features), BF)],
        [((padded, features), F32), ((n_seq, lines, width), F32)],
    )
    later, *w_later = after((inputs, *w_own), weights)
    w_cut = [half for w in w_later for half in jnp.split(w, 2)]
    scale_one = rms_scale(later)
    xhats = gathered((later * scale_one).astype(BF), "seq", seq_steps)
    weights = gathered(weights, "dp", range(1, n_dp))
    weights = [block for weight in weights for block in gathered(weight, "expert", range(1, n_ex))]
    entry_t, gains, exit_t = small_call(
        functools.partial(arrange_kernel, info, n_dp, n_seq, n_ex, share, owned),
        info_row, weights,
        [((3 * width, features), BF), ((2, features), F32), ((features, width), BF)],
        [
            ((group_count, padded, features), BF),
            ((3 * width, features), F32),
            ((features, width), F32),
        ],
    )
    gain_one, gain_two = gains[0:1], gains[1:2]

    inner = 2 if n_seq > 1 and n_seq & (n_seq - 1) == 0 else 1
    in_steps = tuple(range(1, inner))
    out_steps = tuple(range(inner, n_seq, inner))
    w_ups, w_downs = [[w_own[0]]], [[w_own[1]]]
    for step in out_steps:
        cut = [shift(half, "seq", step) for half in w_cut]
        w_ups.append(cut[:2])
        w_downs.append(cut[2:])

    came_upstream = exchanged(send_upstream.reshape(shaped), GROUP).reshape(slots, features)

    (lag,) = after((lag,), send_upstream)
    xfull, qkv, ctx, log = attend(
        info, heads, size, info_row, xhats, gains, entry_t, docs_row, docs_col, lag
    )
    parts = leave(info, n_seq, info_row, ctx, exit_t)

    hidden, scale_two, send_rows = small_call(
        norm_kernel,
        info_row,
        (inputs, gains, place_any, *traded(parts, "seq", seq_steps)),
        [((rows_here, features), F32), ((rows_here, 1), F32), ((slots, features), BF)],
        [],
    )

    came_rows = exchanged(send_rows.reshape(shaped), GROUP).reshape(slots, features)
    rows, ups = [came_rows], [came_upstream]
    for step in in_steps:
        for j in range(2):
            part = slice(j * slots // 2, (j + 1) * slots // 2)
            ups.append(shift(came_upstream[part], "seq", step))
            rows.append(shift(came_rows[part], "seq", step))
    worked = []
    for m in range(1, len(rows)):
        worked.append(expert(rows[m], ups[m], w_ups, w_downs))
    own = []
    for j in range(len(w_ups)):
        own.append(expert(rows[0], ups[0], w_ups[j : j + 1], w_downs[j : j + 1]))
    back_sum = sum(o[0].astype(F32) for o in own)
    for i, step in enumerate(in_steps):
        parts = [shift(worked[2 * i + j][0], "seq", source(n_seq, 0, step)) for j in range(2)]
        back_sum = back_sum + jnp.concatenate(parts).astype(F32)
    back_sum = back_sum.astype(BF)
    returned_back = exchanged(back_sum.reshape(shaped), GROUP).reshape(slots, features)
    own_acts = [o[1][0] for o in own]
    own_bbs = [o[2][0] for o in own]
    groups = [[own_acts]] + [
        [worked[2 * i + j][1] for j in range(2)] for i in range(len(in_steps))
    ]
    results = result(groups, w_downs, came_rows.shape)
    all_acts = [[own_acts[j]] + [w[1][j] for w in worked] for j in range(len(w_ups))]
    all_bbs = [[own_bbs[j]] + [w[2][j] for w in worked] for j in range(len(w_ups))]
    came_ups, came_downs = [], []
    for i, step in enumerate(out_steps):
        step = source(n_seq, 0, step)
        part = expert_grad(rows, all_bbs[i + 1], BF, 2)
        came_ups.append([shift(p, "seq", step) for p in part])
        part = expert_grad(all_acts[i + 1], ups, BF, 2)
        came_downs.append([shift(p, "seq", step) for p in part])

    back_normed_two = dot(place_any, returned_back, 0, 0)
    upper_two = back_normed_two * gain_two
    gain_two_grad = jnp.sum(back_normed_two * hidden * scale_two, axis=0, keepdims=True)
    back_hidden = upstream + scale_two * (
        upper_two
        - hidden * scale_two * scale_two * jnp.mean(upper_two * hidden, axis=1, keepdims=True)
    )
    up_hiddens = gathered(back_hidden.astype(BF), "seq", seq_steps)

    out_sum = handed_back(results, "seq", in_steps).astype(BF)
    returned_out = exchanged(out_sum.reshape(shaped), GROUP).reshape(slots, features)
    block_output = hidden
    for k in range(top_count):
        block_output = block_output + dot(place_each[k], returned_out, 0, 0) * gates[:, k : k + 1]

    up_full, *exit_grads = leave_back(info, n_dp, info_row, up_hiddens, ctx)
    exit_grads = exit_grads[:1] + [
        shift(part, "seq", step)
        for part, step in zip(exit_grads[1:], seq_steps)
    ]
    entry_grad, backs, smalls = attend_back(
        info, heads, size, n_seq, n_dp, n_ex, share, info_row, up_full, exit_t, qkv, log,
        docs_row, docs_col, lag, xfull, gains, entry_t, gain_two_grad, hot_back,
    )

    smalls = traded(smalls, "seq", seq_steps)
    wide = -(-(2 * share + head_count * buckets) // 128) * 128
    assert wide <= features and 2 * share + heads * buckets <= width
    padded = whole_tiles(share + 2) + whole_tiles(owned, 8)
    halves = small_call(
        functools.partial(pack_kernel, info, n_dp, n_seq, n_ex, share, owned),
        info_row,
        (*exit_grads, entry_grad),
        [((n_dp, padded, features), BF)] * n_ex,
        [
            ((n_seq, n_dp, n_ex * share, width), F32),
            ((n_ex, n_dp, padded, features), F32),
        ],
    )
    halves = traded(halves, "expert", range(1, n_ex))
    smalls = small_call(
        functools.partial(small_kernel, info, n_dp, n_seq, n_ex, share, heads, buckets),
        info_row,
        smalls,
        [((n_dp, wide), F32)] * n_ex,
        [((n_seq, n_ex * n_dp, width), F32), ((n_ex, n_dp, wide), F32)],
    )
    smalls = traded(smalls, "expert", range(1, n_ex))
    quarters = small_call(
        functools.partial(fold_kernel, info, n_dp, n_ex, share),
        info_row,
        (*halves, *smalls),
        [((padded, features), BF)] * n_dp,
        [((n_dp, padded, features), F32)],
    )
    folded = quarters
    quarters = traded(quarters, "dp", range(1, n_dp))
    exit_share, small, *pieces = small_call(
        functools.partial(finish_kernel, info, n_dp, share),
        info_row,
        quarters,
        [((share, features), F32), ((1, wide), F32)] + [((chunk, features), F32)] * per,
        [],
    )
    came = [
        lax.ppermute(piece, ALL, tuple((b, a) for a, b in pair))
        for piece, pair in zip(pieces, info.pairs)
    ]
    (entry_share,) = small_call(
        functools.partial(close_kernel, info), info_row, came, [((owned, features), F32)], []
    )
    entry_share, exit_share = entry_share.T, exit_share.T
    small = small[0]
    gain_one_share, gain_two_share = small[:share], small[share : 2 * share]
    bias_total = small[2 * share : 2 * share + head_count * buckets].reshape(head_count, buckets).T

    back_normed_one = summed(backs, "seq", seq_steps)
    upper_one = back_normed_one * gain_one
    back_input = back_hidden + scale_one * (
        upper_one
        - inputs * scale_one * scale_one * jnp.mean(upper_one * inputs, axis=1, keepdims=True)
    )

    own_bb, own_act = after((all_bbs[0][0], all_acts[0][0]), folded)
    (up_grad,) = expert_grad(rows, [own_bb] + all_bbs[0][1:], F32, 1, came_ups)
    (down_grad,) = expert_grad([own_act] + all_acts[0][1:], ups, F32, 1, came_downs)
    return (
        block_output.reshape(block_input.shape),
        back_input.reshape(block_input.shape),
        gain_one_share,
        entry_share,
        exit_share,
        bias_total,
        gain_two_share,
        up_grad[None],
        down_grad[None],
    )


def solution(mesh):
    tokens = P(("dp", "expert"), "seq", None)
    columns = P(None, ALL)
    placed = (
        tokens,
        P(("dp", "expert"), None),
        tokens,
        tokens,
        P(ALL),
        columns,
        columns,
        P(),
        P(ALL),
        P(("dp", "expert"), None, "seq"),
        P(("dp", "expert"), "seq", None),
        tokens,
    )

    return jax.shard_map(
        local,
        mesh=mesh,
        in_specs=placed,
        out_specs=(
            tokens,
            tokens,
            P(ALL),
            columns,
            columns,
            P(),
            P(ALL),
            P(("dp", "expert"), None, "seq"),
            P(("dp", "expert"), "seq", None),
        ),
        check_vma=False,
    )
```
